256 devices in a mesh: comp: 4 (over y), gx: 8 (over x, z_lo), gy: 8 (over z_hi, core).
Axes of the slice: x: 4, y: 4, z: 8 (z_hi: 4, z_lo: 2; z = z_hi * 2 + z_lo), core: 2. Of those that a mesh axis runs over, the one named last changes fastest.
Arguments:
- zonal_flow_speed: float32 [64, 128, 1024], P('comp', 'gx', 'gy'), may hold values from -5 to 5
- meridional_flow_speed: float32 [64, 128, 1024], P('comp', 'gx', 'gy'), may hold values from -5 to 5
- thermal_anomaly: float32 [64, 128, 1024], P('comp', 'gx', 'gy'), may hold values from -6 to 6
- brine_anomaly_values: float32 [64, 128, 1024], P('comp', 'gx', 'gy'), may hold values from -6 to 6
- marine_indicator: int32 [128, 1024], P('gx', 'gy'), may hold values 0 or 1
- seafloor_layer: int32 [128, 1024], P('gx', 'gy'), may hold values from 1 to 64
- dissolved_species: float32 [24, 64, 8, 4, 4, 1024], P(None, None, 'gx', 'comp', None, 'gy'), may hold values from 0.05 to 2
- topmost_sunshine: float32 [8, 4, 4, 1024], P('gx', 'comp', None, 'gy'), may hold values from 0.3 to 3
- attenuation_coefficient: float32 [24], replicated, may hold values from 0.01 to 0.1
- peak_intake_speed: float32 [24], replicated, may hold values from 0.2 to 2
- feedstock_midpoint_constant: float32 [24], replicated, may hold values from 0.05 to 1
- photon_midpoint_constant: float32 [24], replicated, may hold values from 0.05 to 1
- stoichiometry_matrix: float32 [24, 24], replicated, may hold values from -1.25 to 1.25
Outputs:
- east_new: float32 [64, 128, 1024], P('comp', 'gx', 'gy')
- north_new: float32 [64, 128, 1024], P('comp', 'gx', 'gy')
- warmed_result: float32 [64, 128, 1024], P('comp', 'gx', 'gy')
- salt_mixed: float32 [64, 128, 1024], P('comp', 'gx', 'gy')
- buoyancy: float32 [64, 128, 1024], P('comp', 'gx', 'gy')
- result: float32 [24, 64, 8, 4, 4, 1024], P(None, None, 'gx', 'comp', None, 'gy')
The draws below stay inside these ranges and needn't reach their ends.
All inputs are finite; a program needn't handle non-finite values. No bound on the sum of `marine_indicator` on one device may be relied on, other than what follows from the above.
Results may differ from the reference program's by a relative error of at most 0.00007.
Values sent between devices are 32-bit elements; how exact they have to be, the bound alone decides.
A program may use at most 128 MiB of HBM per device.

```python
import math
import jax
import jax.numpy as jnp
from jax import lax

LAYER_COUNT = 64
NTR = 24
SUBX = 4
NSUB = 2
MESH_HEIGHT = 128
MESH_WIDTH = 1024
N_COMP = 4
N_GX = 8


def plant(values, own_key, low, largest):
    longest = values.shape.index(max(values.shape))
    spots = []
    for shift in (0, 1):
        where = [jax.random.randint(jax.random.fold_in(own_key, axis), (), 0, length) for axis, length in enumerate(values.shape)]
        where[longest] = (where[longest] + shift) % values.shape[longest]
        spots.append(tuple(where))
    return values.at[spots[0]].set(low).at[spots[1]].set(largest)


def steps_of(stream_key, extent, shards, smallest, high):
    loudness = 1.0
    for axis_at, parts in shards:
        draws = jax.random.uniform(jax.random.fold_in(jax.random.fold_in(stream_key, 6), axis_at), (parts,), jnp.float32, smallest / len(shards), high / len(shards))
        loudness = loudness * jnp.repeat(jnp.exp(draws), extent[axis_at] // parts).reshape((-1,) + (1,) * (len(extent) - 1 - axis_at))
    return loudness


def bell_draw(stream_key, extent, deviation, reach, split=(), kind=jnp.bfloat16):
    entries = deviation * jax.random.normal(stream_key, extent, jnp.float32)
    if split:
        entries = entries * steps_of(stream_key, extent, split, -0.22, 0.18)
    return jnp.clip(entries, -reach, reach).astype(kind)


def setup_inputs(seed: int = 0) -> dict:
    key_of = jax.random.split(jax.random.key(seed), 14)
    return {
        "zonal_flow_speed": bell_draw(key_of[0], (LAYER_COUNT, MESH_HEIGHT, MESH_WIDTH), 1.0, 5.0, ((0, 4), (1, 8), (2, 8)), jnp.float32),
        "meridional_flow_speed": bell_draw(key_of[1], (LAYER_COUNT, MESH_HEIGHT, MESH_WIDTH), 1.0, 5.0, ((0, 4), (1, 8), (2, 8)), jnp.float32),
        "thermal_anomaly": bell_draw(key_of[2], (LAYER_COUNT, MESH_HEIGHT, MESH_WIDTH), 1.0, 6.0, ((0, 4), (1, 8), (2, 8)), jnp.float32),
        "brine_anomaly_values": bell_draw(key_of[3], (LAYER_COUNT, MESH_HEIGHT, MESH_WIDTH), 1.0, 6.0, ((0, 4), (1, 8), (2, 8)), jnp.float32),
        "marine_indicator": plant((jax.random.randint(key_of[4], (MESH_HEIGHT, MESH_WIDTH), 0, 5) < 4).astype(jnp.int32), jax.random.fold_in(key_of[4], 1), 0, 1),
        "seafloor_layer": plant(jax.random.randint(key_of[5], (MESH_HEIGHT, MESH_WIDTH), 1, LAYER_COUNT + 1), jax.random.fold_in(key_of[5], 1), 1, LAYER_COUNT).astype(jnp.int32),
        "dissolved_species": jnp.clip(jnp.exp(math.log(2.0) - 3.6888794 * jax.random.uniform(key_of[6], (NTR, LAYER_COUNT, N_GX, N_COMP, SUBX, MESH_WIDTH), jnp.float32) ** steps_of(key_of[6], (NTR, LAYER_COUNT, N_GX, N_COMP, SUBX, MESH_WIDTH), ((2, 8), (3, 4), (5, 8)), -0.2, 0.2)), 0.05, 2.0),
        "topmost_sunshine": jnp.clip(jnp.exp(math.log(3.0) - 2.3025851 * jax.random.uniform(key_of[7], (N_GX, N_COMP, SUBX, MESH_WIDTH), jnp.float32) ** steps_of(key_of[7], (N_GX, N_COMP, SUBX, MESH_WIDTH), ((0, 8), (1, 4), (3, 8)), -0.2, 0.2)), 0.3, 3.0),
        "attenuation_coefficient": jnp.clip(jnp.exp(jax.random.uniform(key_of[8], (NTR,), jnp.float32, math.log(0.01), math.log(0.1))), 0.01, 0.1),
        "peak_intake_speed": jnp.clip(jnp.exp(jax.random.uniform(key_of[9], (NTR,), jnp.float32, math.log(0.2), math.log(2.0))), 0.2, 2.0),
        "feedstock_midpoint_constant": jnp.clip(jnp.exp(jax.random.uniform(key_of[10], (NTR,), jnp.float32, math.log(0.05), math.log(1.0))), 0.05, 1.0),
        "photon_midpoint_constant": jnp.clip(jnp.exp(jax.random.uniform(key_of[11], (NTR,), jnp.float32, math.log(0.05), math.log(1.0))), 0.05, 1.0),
        "stoichiometry_matrix": bell_draw(key_of[12], (NTR, NTR), NTR ** -0.5, 1.25, (), jnp.float32),
    }


DT_FLOW = 0.1
CORIOLIS = 0.3
MIXING = 0.15
COURANT = 0.24
DT_BIO = 0.5
WARMING_FACTOR = 0.5
CLEAR_WATER = 0.5
HIGHEST = lax.Precision.HIGHEST


def forward_cell(values, direction):
    widths = [(0, 0)] * values.ndim
    widths[direction] = (0, 1)
    padded_field = jnp.pad(values, widths)
    return lax.slice_in_dim(padded_field, 1, values.shape[direction] + 1, axis=direction)


def backward_cell(values, direction):
    widths = [(0, 0)] * values.ndim
    widths[direction] = (1, 0)
    padded_field = jnp.pad(values, widths)
    return lax.slice_in_dim(padded_field, 0, values.shape[direction], axis=direction)


def reference(zonal_flow_speed, meridional_flow_speed, thermal_anomaly, brine_anomaly_values, marine_indicator, seafloor_layer, dissolved_species, topmost_sunshine, attenuation_coefficient, peak_intake_speed, feedstock_midpoint_constant, photon_midpoint_constant, stoichiometry_matrix):
    depth_index = jnp.arange(LAYER_COUNT, dtype=jnp.int32)[:, None, None]
    submerged_indicator = ((marine_indicator[None] == 1) & (depth_index < seafloor_layer[None])).astype(jnp.float32)
    open_east = submerged_indicator * forward_cell(submerged_indicator, 1)
    open_north = submerged_indicator * forward_cell(submerged_indicator, 2)
    seawater_heaviness = submerged_indicator * (-0.2 * thermal_anomaly + 0.8 * brine_anomaly_values)
    strict_lower = (jnp.arange(LAYER_COUNT)[:, None] > jnp.arange(LAYER_COUNT)[None, :]).astype(jnp.float32)
    depth_above = jnp.dot(strict_lower, seawater_heaviness.reshape(LAYER_COUNT, -1), precision=HIGHEST).reshape(seawater_heaviness.shape)
    weight_of_overlying = depth_above + 0.5 * seawater_heaviness
    east_new = open_east * (zonal_flow_speed + DT_FLOW * (CORIOLIS * meridional_flow_speed - (forward_cell(weight_of_overlying, 1) - weight_of_overlying)))
    north_new = open_north * (meridional_flow_speed + DT_FLOW * (-CORIOLIS * zonal_flow_speed - (forward_cell(weight_of_overlying, 2) - weight_of_overlying)))

    def diapycnal_diffusion(values):
        flux_east = open_east * (forward_cell(values, 1) - values)
        flux_north = open_north * (forward_cell(values, 2) - values)
        return values + MIXING * ((flux_east - backward_cell(flux_east, 1)) + (flux_north - backward_cell(flux_north, 2)))

    thermal_blended = diapycnal_diffusion(thermal_anomaly)
    salt_mixed = diapycnal_diffusion(brine_anomaly_values)
    courant_east = COURANT * jnp.tanh(east_new)
    courant_north = COURANT * jnp.tanh(north_new)
    whole_field = dissolved_species.reshape(NTR, LAYER_COUNT, MESH_HEIGHT, MESH_WIDTH)

    def advect(tracer_field):
        for substep in range(NSUB):
            flux_east = jnp.maximum(courant_east, 0.0) * tracer_field + jnp.minimum(courant_east, 0.0) * forward_cell(tracer_field, 1)
            flux_north = jnp.maximum(courant_north, 0.0) * tracer_field + jnp.minimum(courant_north, 0.0) * forward_cell(tracer_field, 2)
            tracer_field = submerged_indicator * (tracer_field - (flux_east - backward_cell(flux_east, 1)) - (flux_north - backward_cell(flux_north, 2)))
        return tracer_field

    advected = lax.map(advect, whole_field)
    layer_depth = 2.0 / LAYER_COUNT
    optical_step = layer_depth * (CLEAR_WATER + jnp.tensordot(attenuation_coefficient, advected, axes=1, precision=HIGHEST))
    optical_above = jnp.dot(strict_lower, optical_step.reshape(LAYER_COUNT, -1), precision=HIGHEST).reshape(optical_step.shape)
    transmitted = jnp.exp(-optical_above)
    surface = topmost_sunshine.reshape(MESH_HEIGHT, MESH_WIDTH)[None]
    light_level = surface * transmitted * jnp.exp(-0.5 * optical_step)
    warming_step = submerged_indicator * surface * transmitted * (1.0 - jnp.exp(-optical_step)) / layer_depth
    nutrient = advected[0]

    def uptake(inputs):
        tracer_field, rate_max, nutrient_half, light_sat = inputs
        return rate_max * (nutrient / (nutrient_half + nutrient)) * (light_level / (light_level + light_sat)) * tracer_field

    uptake_rates = lax.map(uptake, (advected, peak_intake_speed, feedstock_midpoint_constant, photon_midpoint_constant))
    change = jnp.tensordot(stoichiometry_matrix, uptake_rates, axes=1, precision=HIGHEST)
    result = advected + DT_BIO * submerged_indicator * change
    warmed_result = thermal_blended + WARMING_FACTOR * warming_step
    buoyancy = submerged_indicator * (0.2 * warmed_result - 0.8 * salt_mixed)
    return east_new, north_new, warmed_result, salt_mixed, buoyancy, result.reshape(dissolved_species.shape)
```

```python
import functools

import jax
import jax.numpy as jnp
from jax import lax
from jax.experimental import pallas as pl
from jax.experimental.pallas import tpu as pltpu
from jax.sharding import PartitionSpec as P

MESH = pl.DeviceIdType.MESH
LANES = 128
GROUP = 8

DT_FLOW = 0.1
CORIOLIS = 0.3
MIXING = 0.15
COURANT = 0.24
DT_BIO = 0.5
WARMING_FACTOR = 0.5
CLEAR_WATER = 0.5


def ocean_kernel(
    dims,
    zonal_ref,
    merid_ref,
    therm_ref,
    brine_ref,
    mask_ref,
    bottom_ref,
    tracer_ref,
    sun_ref,
    absorb_ref,
    growth_ref,
    half_ref,
    light_half_ref,
    stoich_ref,
    east_out,
    north_out,
    warmed_out,
    salt_out,
    buoy_out,
    result_out,
    fld,
    fldh,
    mb,
    mby,
    wet,
    weth,
    den,
    denh,
    tot,
    prs,
    prsh,
    vel,
    cour_e,
    cour_n,
    cour_p,
    cer,
    cnr,
    cpr,
    cps,
    cpack,
    mixed,
    heat,
    fin,
    q0,
    q1,
    res,
    lo,
    hi,
    hsend,
    hrecv,
    coef,
    wcol,
    warm,
    carry,
    upt,
    lsem,
    osem,
    p1s,
    p1r,
    cs_s,
    cs_r,
    ts_s,
    ts_r,
    as_s,
    as_r,
    qs_s,
    qs_r,
    hs_s,
    hs_r,
    ws_s,
    ws_r,
):
    ntr, levels, rows, lev, sub, ng, ny = dims
    nchunk = levels // GROUP
    nc = levels // lev
    c, g, y = lax.axis_index("comp"), lax.axis_index("gx"), lax.axis_index("gy")
    up = {
        "comp": lax.rem(c + 1, nc),
        "gx": jnp.where(c == nc - 1, lax.rem(g + 1, ng), g),
        "gy": y,
    }
    down = {
        "comp": lax.rem(c + nc - 1, nc),
        "gx": jnp.where(c == 0, lax.rem(g + ng - 1, ng), g),
        "gy": y,
    }
    gxp = {"comp": c, "gx": lax.rem(g + 1, ng), "gy": y}
    gxm = {"comp": c, "gx": lax.rem(g + ng - 1, ng), "gy": y}
    gyp = {"comp": c, "gx": g, "gy": lax.rem(y + 1, ny)}
    gym = {"comp": c, "gx": g, "gy": lax.rem(y + ny - 1, ny)}
    peers = [{"comp": lax.rem(c + d, nc), "gx": g, "gy": y} for d in range(1, nc)]

    def remote(src, dst, send, recv, device):
        return pltpu.make_async_remote_copy(
            src_ref=src,
            dst_ref=dst,
            send_sem=send,
            recv_sem=recv,
            device_id=device,
            device_id_type=MESH,
        )

    def chunk(k):
        return pl.ds(pl.multiple_of(k * GROUP, GROUP), GROUP)

    fields = (zonal_ref, merid_ref, therm_ref, brine_ref)

    def load_rows(r, _):
        for f, ref in enumerate(fields):
            pltpu.make_async_copy(ref.at[:, r, 0, :], fld.at[f, r + 1], lsem.at[f]).start()
        return 0

    lax.fori_loop(0, rows, load_rows, 0)
    for i, ref in enumerate((mask_ref, bottom_ref)):
        pltpu.make_async_copy(ref, mb.at[i, pl.ds(1, rows)], lsem.at[4 + i]).start()

    def load_tracers(k, _):
        for r in range(sub):
            pltpu.make_async_copy(
                tracer_ref.at[:, chunk(k), r, 0, :], q0.at[:, r, chunk(k), :], lsem.at[6 + k]
            ).start()
        return 0

    lax.fori_loop(0, nchunk, load_tracers, 0)

    barrier = pltpu.get_barrier_semaphore()
    partners = [up, down, gxp, gxm, gyp, gym] + peers
    for device in partners:
        pl.semaphore_signal(barrier, inc=1, device_id=device, device_id_type=MESH)
    pl.semaphore_wait(barrier, len(partners))

    first = []
    for f, ref in enumerate(fields):
        first.append((ref.at[:, rows - 1, 0, :], fld.at[f, 0], gxp))
    for f in (2, 3):
        first.append((fields[f].at[:, 0, 0, :], fld.at[f, rows + 1], gxm))
    for i, ref in enumerate((mask_ref, bottom_ref)):
        first.append((ref.at[pl.ds(rows - 1, 1)], mb.at[i, pl.ds(0, 1)], gxp))
        first.append((ref.at[pl.ds(0, 1)], mb.at[i, pl.ds(rows + 1, 1)], gxm))
        first.append((ref, mby.at[0, i], gyp))
        first.append((ref, mby.at[1, i], gym))
    first = [
        remote(src, dst, p1s.at[n], p1r.at[n], device)
        for n, (src, dst, device) in enumerate(first)
    ]
    for copy in first:
        copy.start()

    def edge_copies(stage, k):
        if stage == 0:
            top = tracer_ref.at[:, chunk(k), sub - 1, 0, :]
            low = tracer_ref.at[:, chunk(k), 0, 0, :]
        else:
            top = q1.at[:, sub - 1, chunk(k), :]
            low = q1.at[:, 0, chunk(k), :]
        return (
            remote(
                top, lo.at[stage, :, chunk(k), :], qs_s.at[stage, 0, k], qs_r.at[stage, 0, k], up
            ),
            remote(
                low, hi.at[stage, :, chunk(k), :], qs_s.at[stage, 1, k], qs_r.at[stage, 1, k], down
            ),
        )

    def send_edges(stage, k):
        for copy in edge_copies(stage, k):
            copy.start()

    def side_copies(stage, k):
        return (
            remote(
                hsend.at[stage, :, chunk(k), :],
                hrecv.at[stage, 0, :, chunk(k), :],
                hs_s.at[stage, 0, k],
                hs_r.at[stage, 0, k],
                gyp,
            ),
            remote(
                hsend.at[stage, :, chunk(k), :],
                hrecv.at[stage, 1, :, chunk(k), :],
                hs_s.at[stage, 1, k],
                hs_r.at[stage, 1, k],
                gym,
            ),
        )

    def send_sides(stage, k):
        for copy in side_copies(stage, k):
            copy.start()

    send_edges(0, 0)
    send_edges(0, 1)

    lane16 = lax.broadcasted_iota(jnp.int32, (lev, LANES), 1)
    level16 = lax.broadcasted_iota(jnp.int32, (lev, LANES), 0)
    depth16 = (level16 + c * lev).astype(jnp.float32)
    lane8 = lax.broadcasted_iota(jnp.int32, (GROUP, LANES), 1)
    level8 = lax.broadcasted_iota(jnp.int32, (GROUP, LANES), 0)

    def merged(ahead, behind, lanes):
        return jnp.where((lanes & 1) == 1, ahead, pltpu.roll(behind, 2, 1))

    def slot_of(both, m):
        return pltpu.roll(both, (126 - m) % LANES, 1)

    def packed(acc, x, m, lanes):
        return jnp.where((lanes >> 1) == (m >> 1), pltpu.roll(x, (m + 1) % LANES, 1), acc)

    def ahead_of(x, h, lanes):
        return jnp.where(lanes == LANES - 1, h, pltpu.roll(x, LANES - 1, 1))

    def behind_of(x, h, lanes):
        return jnp.where(lanes == 0, h, pltpu.roll(x, 1, 1))

    for f in range(4):
        pltpu.make_async_copy(fld.at[f, pl.ds(1, rows)], fld.at[f, pl.ds(1, rows)], lsem.at[f]).wait()
    acc = jnp.zeros((lev, LANES), jnp.float32)
    for r in range(rows):
        for f in range(4):
            acc = packed(acc, fld[f, r + 1], 8 * r + 2 * f, lane16)
    cps[...] = acc
    column_copies = (
        remote(cps, cpack.at[0], cs_s.at[0], cs_r.at[0], gyp),
        remote(cps, cpack.at[1], cs_s.at[1], cs_r.at[1], gym),
    )
    for copy in column_copies:
        copy.start()

    for i, ref in enumerate((mask_ref, bottom_ref)):
        pltpu.make_async_copy(ref, mb.at[i, pl.ds(1, rows)], lsem.at[4 + i]).wait()

    def reach(m, b):
        return jnp.where(m == 1, b, 0).astype(jnp.float32)

    def wet_row(e, valid):
        depth = reach(mb[0, e], mb[1, e])
        if valid is not None:
            depth = jnp.where(valid, depth, 0.0)
        w = jnp.where(depth16 < depth, 1.0, 0.0)
        d = w * (-0.2 * fld[2, e] + 0.8 * fld[3, e])
        wet[e] = w
        den[e] = d
        tot[c, e] = jnp.sum(d, axis=0, keepdims=True)

    def own_row(r, _):
        wet_row(r + 1, None)
        return 0

    lax.fori_loop(0, rows, own_row, 0)

    def pack_sides(k, _):
        pltpu.make_async_copy(
            q0.at[:, :, chunk(k), :], q0.at[:, :, chunk(k), :], lsem.at[6 + k]
        ).wait()
        for pair in range(sub // 2):
            a = jnp.zeros((GROUP, LANES), jnp.float32)
            for half in range(2):
                for t in range(ntr):
                    a = packed(a, q0[t, 2 * pair + half, chunk(k), :], 64 * half + 2 * t, lane8)
            hsend[0, pair, chunk(k), :] = a
        send_sides(0, k)
        return 0

    lax.fori_loop(0, nchunk, pack_sides, 0)

    for copy in first:
        copy.wait_recv()
    for copy in column_copies:
        copy.wait_recv()
    wet_row(0, g > 0)
    wet_row(rows + 1, g < ng - 1)
    both = merged(cpack[1], cpack[0], lane16)
    for r in range(rows):
        for f in range(4):
            fldh[f, r] = slot_of(both, 8 * r + 2 * f)

    def halo_columns(r, _):
        behind = jnp.broadcast_to(reach(mby[0, 0, r], mby[0, 1, r]), (lev, LANES))
        ahead = jnp.broadcast_to(reach(mby[1, 0, r], mby[1, 1, r]), (lev, LANES))
        behind = jnp.where(y > 0, pltpu.roll(behind, 1, 1), 0.0)
        ahead = jnp.where(y < ny - 1, pltpu.roll(ahead, LANES - 1, 1), 0.0)
        depth = jnp.where(lane16 == 0, behind, ahead)
        w = jnp.where(depth16 < depth, 1.0, 0.0)
        d = w * (-0.2 * fldh[2, r] + 0.8 * fldh[3, r])
        weth[r] = w
        denh[r] = d
        tot[c, rows + 2 + r] = jnp.sum(d, axis=0, keepdims=True)
        return 0

    lax.fori_loop(0, rows, halo_columns, 0)
    total_copies = [
        remote(tot.at[c], tot.at[c], ts_s.at[d], ts_r.at[d], peer) for d, peer in enumerate(peers)
    ]
    for copy in total_copies:
        copy.start()
    send_edges(0, 2)
    send_edges(0, 3)

    def mixing_row(r, _):
        w, h = wet[r + 1], weth[r]
        open_e, open_w = w * wet[r + 2], wet[r] * w
        open_n, open_s = w * ahead_of(w, h, lane16), w * behind_of(w, h, lane16)
        for i in range(2):
            x, xh = fld[2 + i, r + 1], fldh[2 + i, r]
            flux_e = open_e * (fld[2 + i, r + 2] - x)
            flux_w = open_w * (x - fld[2 + i, r])
            flux_n = open_n * (ahead_of(x, xh, lane16) - x)
            flux_s = open_s * (x - behind_of(x, xh, lane16))
            mixed[i, r] = x + MIXING * ((flux_e - flux_w) + (flux_n - flux_s))
        return 0

    lax.fori_loop(0, rows, mixing_row, 0)

    for d, peer in enumerate(peers):
        total_copies[d].wait_recv()

    def pressure_of(d, e):
        incl = d
        step = 1
        while step < lev:
            incl = incl + jnp.where(level16 >= step, pltpu.roll(incl, step, 0), 0.0)
            step *= 2
        offset = jnp.zeros((1, LANES), jnp.float32)
        for p in range(nc - 1):
            offset = offset + jnp.where(p < c, tot[p, e], 0.0)
        return offset + incl - 0.5 * d

    def pressure_row(e, _):
        prs[e] = pressure_of(den[e], e)
        return 0

    def pressure_column(r, _):
        prsh[r] = pressure_of(denh[r], rows + 2 + r)
        return 0

    lax.fori_loop(0, rows + 2, pressure_row, 0)
    lax.fori_loop(0, rows, pressure_column, 0)

    def east_row(e, _):
        v = (wet[e] * wet[e + 1]) * (
            fld[0, e] + DT_FLOW * (CORIOLIS * fld[1, e] - (prs[e + 1] - prs[e]))
        )
        vel[0, e] = v
        cour_e[e] = COURANT * jnp.tanh(v)
        return 0

    lax.fori_loop(0, rows + 1, east_row, 0)

    def north_group(p, _):
        pack = jnp.zeros((lev, LANES), jnp.float32)
        for i in range(sub):
            r = sub * p + i
            w, h, ps, ph = wet[r + 1], weth[r], prs[r + 1], prsh[r]
            v = (w * ahead_of(w, h, lane16)) * (
                fld[1, r + 1]
                + DT_FLOW * (-CORIOLIS * fld[0, r + 1] - (ahead_of(ps, ph, lane16) - ps))
            )
            vel[1, r + 1] = v
            cour_n[r] = COURANT * jnp.tanh(v)
            before = (w * h) * (
                fldh[1, r] + DT_FLOW * (-CORIOLIS * fldh[0, r] - (ps - ph))
            )
            pack = jnp.where(
                lane16 == i, jnp.broadcast_to(before[:, 0:1], (lev, LANES)), pack
            )
        cour_p[p] = COURANT * jnp.tanh(pack)
        return 0

    lax.fori_loop(0, nc, north_group, 0)

    mine = pl.ds(pl.multiple_of(c * lev, lev), lev)
    velocity_copies = []
    for d, peer in enumerate(peers):
        p = peer["comp"]
        for n, (src, dst) in enumerate(
            (
                (cour_e.at[pl.ds(sub * p, sub + 1)], cer.at[:, mine, :]),
                (cour_n.at[pl.ds(sub * p, sub)], cnr.at[:, mine, :]),
                (cour_p.at[p], cpr.at[mine, :]),
            )
        ):
            velocity_copies.append(remote(src, dst, as_s.at[d, n], as_r.at[d, n], peer))
    for copy in velocity_copies:
        copy.start()
    for k in range(4, nchunk):
        send_edges(0, k)
    for i in range(sub + 1):
        cer[i, mine, :] = cour_e[sub * c + i]
    for i in range(sub):
        cnr[i, mine, :] = cour_n[sub * c + i]
    cpr[mine, :] = cour_p[c]

    def store_rows(r, _):
        pltpu.make_async_copy(vel.at[0, r + 1], east_out.at[:, r, 0, :], osem.at[0]).start()
        pltpu.make_async_copy(vel.at[1, r + 1], north_out.at[:, r, 0, :], osem.at[1]).start()
        pltpu.make_async_copy(mixed.at[1, r], salt_out.at[:, r, 0, :], osem.at[2]).start()
        return 0

    lax.fori_loop(0, rows, store_rows, 0)

    for copy in velocity_copies:
        copy.wait_recv()

    def wet_chunk(k, r):
        depth = reach(mb[0, sub * c + r + 1], mb[1, sub * c + r + 1])
        return jnp.where((level8 + k * GROUP).astype(jnp.float32) < depth, 1.0, 0.0)

    def coefficients(k):
        for r in range(sub):
            ce, cw, cn = cer[r + 1, chunk(k), :], cer[r, chunk(k), :], cnr[r, chunk(k), :]
            edge = cpr[chunk(k), :]
            if r:
                edge = pltpu.roll(edge, LANES - r, 1)
            cs = behind_of(cn, edge, lane8)
            w = wet_chunk(k, r)
            out_e, in_e = jnp.maximum(ce, 0.0), jnp.minimum(ce, 0.0)
            out_w, in_w = jnp.maximum(cw, 0.0), jnp.minimum(cw, 0.0)
            out_n, in_n = jnp.maximum(cn, 0.0), jnp.minimum(cn, 0.0)
            out_s, in_s = jnp.maximum(cs, 0.0), jnp.minimum(cs, 0.0)
            wcol[r, chunk(k), :] = w
            coef[0, r, chunk(k), :] = w * (1.0 - (out_e - in_w) - (out_n - in_s))
            coef[1, r, chunk(k), :] = -w * in_e
            coef[2, r, chunk(k), :] = w * out_w
            coef[3, r, chunk(k), :] = -w * in_n
            coef[4, r, chunk(k), :] = w * out_s

    def substep(k, src, dst, stage, each):
        cf = [[coef[i, r, chunk(k), :] for i in range(5)] for r in range(sub)]
        both = [
            merged(hrecv[stage, 1, p, chunk(k), :], hrecv[stage, 0, p, chunk(k), :], lane8)
            for p in range(sub // 2)
        ]
        for t in range(ntr):
            q = [lo[stage, t, chunk(k), :]]
            q += [src[t, r, chunk(k), :] for r in range(sub)]
            q += [hi[stage, t, chunk(k), :]]
            for r in range(sub):
                x = q[r + 1]
                h = slot_of(both[r // 2], 64 * (r % 2) + 2 * t)
                new = (
                    cf[r][0] * x
                    + cf[r][1] * q[r + 2]
                    + cf[r][2] * q[r]
                    + cf[r][3] * ahead_of(x, h, lane8)
                    + cf[r][4] * behind_of(x, h, lane8)
                )
                dst[t, r, chunk(k), :] = new
                each(t, r, new)

    def first_substep(k, _):
        for copy in edge_copies(0, k):
            copy.wait_recv()
        for copy in side_copies(0, k):
            copy.wait_recv()
        coefficients(k)
        packs = [jnp.zeros((GROUP, LANES), jnp.float32) for _ in range(sub // 2)]

        def each(t, r, new):
            packs[r // 2] = packed(packs[r // 2], new, 64 * (r % 2) + 2 * t, lane8)

        substep(k, q0, q1, 0, each)
        for p in range(sub // 2):
            hsend[1, p, chunk(k), :] = packs[p]
        send_edges(1, k)
        send_sides(1, k)
        return 0

    lax.fori_loop(0, nchunk, first_substep, 0)

    layer = 2.0 / levels
    block = 4
    carry[...] = jnp.zeros_like(carry)

    def second_substep(k):
        for copy in edge_copies(1, k):
            copy.wait_recv()
        for copy in side_copies(1, k):
            copy.wait_recv()
        optical = [jnp.zeros((GROUP, LANES), jnp.float32) for _ in range(sub)]

        def each(t, r, new):
            optical[r] = optical[r] + absorb_ref[t] * new

        substep(k, q1, q0, 1, each)
        light, scaled, nutrient = [], [], []
        for r in range(sub):
            step = layer * (CLEAR_WATER + optical[r])
            above = jnp.where(level8 >= 1, pltpu.roll(step, 1, 0), 0.0)
            for d in (1, 2, 4):
                above = above + jnp.where(level8 >= d, pltpu.roll(above, d, 0), 0.0)
            before = carry[r]
            carry[r] = before + jnp.sum(step, axis=0, keepdims=True)
            arriving = sun_ref[r] * jnp.exp(-(before + above))
            warm[r, chunk(k), :] = (
                wcol[r, chunk(k), :] * arriving * (1.0 - jnp.exp(-step)) / layer
            )
            light.append(arriving * jnp.exp(-0.5 * step))
            nutrient.append(q0[0, r, chunk(k), :])
            scaled.append(nutrient[r] * light[r])
        for t in range(ntr):
            for r in range(sub):
                below = (half_ref[t] + nutrient[r]) * (light[r] + light_half_ref[t])
                upt[t, r] = (growth_ref[t] * scaled[r]) * q0[t, r, chunk(k), :] / below
        half_wet = [DT_BIO * wcol[r, chunk(k), :] for r in range(sub)]

        def react(b, _):
            sums = [[jnp.zeros((GROUP, LANES), jnp.float32)] * sub for _ in range(block)]
            for t in range(ntr):
                u = [upt[t, r] for r in range(sub)]
                for i in range(block):
                    s = stoich_ref[block * b + i, t]
                    sums[i] = [sums[i][r] + s * u[r] for r in range(sub)]
            for i in range(block):
                for r in range(sub):
                    res[block * b + i, r, chunk(k), :] = (
                        q0[block * b + i, r, chunk(k), :] + half_wet[r] * sums[i][r]
                    )
            return 0

        lax.fori_loop(0, ntr // block, react, 0)
        for r in range(sub):
            pltpu.make_async_copy(
                res.at[:, r, chunk(k), :], result_out.at[:, chunk(k), r, 0, :], osem.at[3]
            ).start()

    def heat_copy(p):
        part = pl.ds(pl.multiple_of(p * lev, lev), lev)
        return remote(
            warm.at[:, part, :],
            heat.at[pl.ds(sub * c, sub)],
            ws_s.at[p],
            ws_r.at[c],
            {"comp": p, "gx": g, "gy": y},
        )

    def group_of_levels(p, _):
        def one(i, _):
            second_substep(p * (lev // GROUP) + i)
            return 0

        lax.fori_loop(0, lev // GROUP, one, 0)

        @pl.when(p != c)
        def _():
            heat_copy(p).start()

        @pl.when(p == c)
        def _():
            part = pl.ds(pl.multiple_of(p * lev, lev), lev)
            for r in range(sub):
                heat[sub * c + r] = warm[r, part, :]

        return 0

    lax.fori_loop(0, nc, group_of_levels, 0)

    for d in range(1, nc):
        p = lax.rem(c + nc - d, nc)
        remote(
            warm.at[:, pl.ds(0, lev), :],
            heat.at[pl.ds(sub * p, sub)],
            ws_s.at[p],
            ws_r.at[p],
            {"comp": p, "gx": g, "gy": y},
        ).wait_recv()

    def final_row(r, _):
        warmed = mixed[0, r] + WARMING_FACTOR * heat[r]
        fin[0, r] = warmed
        fin[1, r] = wet[r + 1] * (0.2 * warmed - 0.8 * mixed[1, r])
        return 0

    lax.fori_loop(0, rows, final_row, 0)

    def store_final(r, _):
        pltpu.make_async_copy(fin.at[0, r], warmed_out.at[:, r, 0, :], osem.at[4]).start()
        pltpu.make_async_copy(fin.at[1, r], buoy_out.at[:, r, 0, :], osem.at[5]).start()
        return 0

    lax.fori_loop(0, rows, store_final, 0)

    for copy in first + list(column_copies) + total_copies + velocity_copies:
        copy.wait_send()

    def drain(k, _):
        for stage in range(2):
            for copy in edge_copies(stage, k) + side_copies(stage, k):
                copy.wait_send()
        return 0

    lax.fori_loop(0, nchunk, drain, 0)
    for d in range(1, nc):
        heat_copy(lax.rem(c + d, nc)).wait_send()
    for n, ref in enumerate(
        (vel.at[0, pl.ds(1, rows)], vel.at[1, pl.ds(1, rows)], mixed.at[1], res, fin.at[0], fin.at[1])
    ):
        pltpu.make_async_copy(ref, ref, osem.at[n]).wait()


def on_device(mesh_shape, *args):
    (
        zonal,
        merid,
        therm,
        brine,
        mask,
        bottom,
        tracers,
        sun,
        absorb,
        growth,
        half,
        light_half,
        stoich,
    ) = args
    lev, rows, lanes = zonal.shape
    ntr, levels, sub = tracers.shape[0], tracers.shape[1], tracers.shape[4]
    nc, ng, ny = mesh_shape
    nchunk = levels // GROUP
    f32, i32 = jnp.float32, jnp.int32
    column = (lev, rows, 1, lanes)
    vm, dma = pltpu.VMEM, pltpu.SemaphoreType.DMA
    anywhere = pl.BlockSpec(memory_space=pl.ANY)
    in_vmem = pl.BlockSpec(memory_space=pltpu.VMEM)
    in_smem = pl.BlockSpec(memory_space=pltpu.SMEM)
    scratch = [
        vm((4, rows + 2, lev, lanes), f32),
        vm((4, rows, lev, lanes), f32),
        vm((2, rows + 2, 1, lanes), i32),
        vm((2, 2, rows, 1, lanes), i32),
        vm((rows + 2, lev, lanes), f32),
        vm((rows, lev, lanes), f32),
        vm((rows + 2, lev, lanes), f32),
        vm((rows, lev, lanes), f32),
        vm((nc, 2 * rows + 2, 1, lanes), f32),
        vm((rows + 2, lev, lanes), f32),
        vm((rows, lev, lanes), f32),
        vm((2, rows + 1, lev, lanes), f32),
        vm((rows + 1, lev, lanes), f32),
        vm((rows, lev, lanes), f32),
        vm((nc, lev, lanes), f32),
        vm((sub + 1, levels, lanes), f32),
        vm((sub, levels, lanes), f32),
        vm((levels, lanes), f32),
        vm((lev, lanes), f32),
        vm((2, lev, lanes), f32),
        vm((2, rows, lev, lanes), f32),
        vm((rows, lev, lanes), f32),
        vm((2, rows, lev, lanes), f32),
        vm((ntr, sub, levels, lanes), f32),
        vm((ntr, sub, levels, lanes), f32),
        vm((ntr, sub, levels, lanes), f32),
        vm((2, ntr, levels, lanes), f32),
        vm((2, ntr, levels, lanes), f32),
        vm((2, sub // 2, levels, lanes), f32),
        vm((2, 2, sub // 2, levels, lanes), f32),
        vm((5, sub, levels, lanes), f32),
        vm((sub, levels, lanes), f32),
        vm((sub, levels, lanes), f32),
        vm((sub, GROUP, lanes), f32),
        vm((ntr, sub, GROUP, lanes), f32),
        dma((6 + nchunk,)),
        dma((6,)),
        dma((14,)),
        dma((14,)),
        dma((2,)),
        dma((2,)),
        dma((nc - 1,)),
        dma((nc - 1,)),
        dma((nc - 1, 3)),
        dma((nc - 1, 3)),
        dma((2, 2, nchunk)),
        dma((2, 2, nchunk)),
        dma((2, 2, nchunk)),
        dma((2, 2, nchunk)),
        dma((nc,)),
        dma((nc,)),
    ]
    outs = pl.pallas_call(
        functools.partial(ocean_kernel, (ntr, levels, rows, lev, sub, ng, ny)),
        out_shape=[jax.ShapeDtypeStruct(column, f32)] * 5
        + [jax.ShapeDtypeStruct((ntr, levels, sub, 1, lanes), f32)],
        in_specs=[anywhere] * 7 + [in_vmem] + [in_smem] * 5,
        out_specs=[anywhere] * 6,
        scratch_shapes=scratch,
        compiler_params=pltpu.CompilerParams(
            collective_id=0, has_side_effects=True, vmem_limit_bytes=48 << 20
        ),
        name="ocean",
    )(
        *(x.reshape(column) for x in (zonal, merid, therm, brine)),
        mask.reshape(rows, 1, lanes),
        bottom.reshape(rows, 1, lanes),
        tracers.reshape(ntr, levels, sub, 1, lanes),
        sun.reshape(sub, 1, lanes),
        absorb,
        growth,
        half,
        light_half,
        stoich,
    )
    return tuple(x.reshape(zonal.shape) for x in outs[:5]) + (outs[5].reshape(tracers.shape),)


def solution(mesh):
    field = P("comp", "gx", "gy")
    tile = P("gx", "gy")
    tracer = P(None, None, "gx", "comp", None, "gy")
    shape = tuple(mesh.shape[a] for a in ("comp", "gx", "gy"))
    return jax.shard_map(
        functools.partial(on_device, shape),
        mesh=mesh,
        in_specs=(field,) * 4 + (tile,) * 2 + (tracer, P("gx", "comp", None, "gy")) + (P(),) * 5,
        out_specs=(field,) * 5 + (tracer,),
        check_vma=False,
    )
```

```python
import functools

import jax
import jax.numpy as jnp
from jax import lax
from jax.experimental import pallas as pl
from jax.experimental.pallas import tpu as pltpu
from jax.sharding import PartitionSpec as P

MESH = pl.DeviceIdType.MESH
LANES = 128
GROUP = 8
DEPTH = 2

DT_FLOW = 0.1
CORIOLIS = 0.3
MIXING = 0.15
COURANT = 0.24
DT_BIO = 0.5
WARMING_FACTOR = 0.5
CLEAR_WATER = 0.5


def ocean_kernel(
    dims,
    zonal_ref,
    merid_ref,
    therm_ref,
    brine_ref,
    mask_ref,
    bottom_ref,
    tracer_ref,
    sun_in,
    absorb_in,
    growth_in,
    half_in,
    light_half_in,
    stoich_in,
    east_out,
    north_out,
    warmed_out,
    salt_out,
    buoy_out,
    result_out,
    fld,
    fldh,
    mb,
    mby,
    wet,
    weth,
    den,
    denh,
    tot,
    prs,
    prsh,
    vel,
    cour_e,
    cour_n,
    cour_p,
    cer,
    cnr,
    cpr,
    cps,
    cpack,
    mixed,
    heat,
    fin,
    q0,
    q1,
    res,
    lo,
    hi,
    hsend,
    hrecv,
    coef,
    wcol,
    warm,
    carry,
    upt,
    sun_ref,
    absorb_ref,
    growth_ref,
    half_ref,
    light_half_ref,
    stoich_ref,
    lsem,
    osem,
    p1s,
    p1r,
    cs_s,
    cs_r,
    ts_s,
    ts_r,
    as_s,
    as_r,
    qs_s,
    qs_r,
    hs_s,
    hs_r,
    ws_s,
    ws_r,
):
    ntr, levels, rows, lev, sub, ng, ny = dims
    nchunk = levels // GROUP
    nc = levels // lev
    c, g, y = lax.axis_index("comp"), lax.axis_index("gx"), lax.axis_index("gy")
    up = {
        "comp": lax.rem(c + 1, nc),
        "gx": jnp.where(c == nc - 1, lax.rem(g + 1, ng), g),
        "gy": y,
    }
    down = {
        "comp": lax.rem(c + nc - 1, nc),
        "gx": jnp.where(c == 0, lax.rem(g + ng - 1, ng), g),
        "gy": y,
    }
    gxp = {"comp": c, "gx": lax.rem(g + 1, ng), "gy": y}
    gxm = {"comp": c, "gx": lax.rem(g + ng - 1, ng), "gy": y}
    gyp = {"comp": c, "gx": g, "gy": lax.rem(y + 1, ny)}
    gym = {"comp": c, "gx": g, "gy": lax.rem(y + ny - 1, ny)}
    peers = [{"comp": lax.rem(c + d, nc), "gx": g, "gy": y} for d in range(1, nc)]

    def remote(src, dst, send, recv, device):
        return pltpu.make_async_remote_copy(
            src_ref=src,
            dst_ref=dst,
            send_sem=send,
            recv_sem=recv,
            device_id=device,
            device_id_type=MESH,
        )

    def chunk(k):
        return pl.ds(pl.multiple_of(k * GROUP, GROUP), GROUP)

    barrier = pltpu.get_barrier_semaphore()
    partners = [up, down, gxp, gxm, gyp, gym] + peers
    for device in partners:
        pl.semaphore_signal(barrier, inc=1, device_id=device, device_id_type=MESH)

    fields = (zonal_ref, merid_ref, therm_ref, brine_ref)

    def load_rows(r, _):
        for f, ref in enumerate(fields):
            pltpu.make_async_copy(ref.at[:, r, 0, :], fld.at[f, r + 1], lsem.at[f]).start()
        return 0

    lax.fori_loop(0, rows, load_rows, 0)
    for i, ref in enumerate((mask_ref, bottom_ref)):
        pltpu.make_async_copy(ref, mb.at[i, pl.ds(1, rows)], lsem.at[4 + i]).start()

    def load_tracers(k, _):
        for r in range(sub):
            pltpu.make_async_copy(
                tracer_ref.at[:, chunk(k), r, 0, :], q0.at[:, r, chunk(k), :], lsem.at[6 + k]
            ).start()
        return 0

    lax.fori_loop(0, nchunk, load_tracers, 0)
    settings = [
        pltpu.make_async_copy(src, dst, lsem.at[6 + nchunk + n])
        for n, (src, dst) in enumerate(
            (
                (sun_in, sun_ref),
                (absorb_in, absorb_ref),
                (growth_in, growth_ref),
                (half_in, half_ref),
                (light_half_in, light_half_ref),
                (stoich_in, stoich_ref),
            )
        )
    ]
    for copy in settings:
        copy.start()

    pl.semaphore_wait(barrier, len(partners))

    first = []
    for f, ref in enumerate(fields):
        first.append((ref.at[:, rows - 1, 0, :], fld.at[f, 0], gxp))
    for f in (2, 3):
        first.append((fields[f].at[:, 0, 0, :], fld.at[f, rows + 1], gxm))
    for i, ref in enumerate((mask_ref, bottom_ref)):
        first.append((ref.at[pl.ds(rows - 1, 1)], mb.at[i, pl.ds(0, 1)], gxp))
        first.append((ref.at[pl.ds(0, 1)], mb.at[i, pl.ds(rows + 1, 1)], gxm))
        first.append((ref, mby.at[0, i], gyp))
        first.append((ref, mby.at[1, i], gym))
    first = [
        remote(src, dst, p1s.at[n], p1r.at[n], device)
        for n, (src, dst, device) in enumerate(first)
    ]
    for copy in first:
        copy.start()

    def edge_copies(stage, k):
        if stage == 0:
            top = tracer_ref.at[:, chunk(k), sub - 1, 0, :]
            low = tracer_ref.at[:, chunk(k), 0, 0, :]
        else:
            top = q1.at[:, sub - 1, chunk(k), :]
            low = q1.at[:, 0, chunk(k), :]
        return (
            remote(
                top, lo.at[stage, :, chunk(k), :], qs_s.at[stage, 0, k], qs_r.at[stage, 0, k], up
            ),
            remote(
                low, hi.at[stage, :, chunk(k), :], qs_s.at[stage, 1, k], qs_r.at[stage, 1, k], down
            ),
        )

    def send_edges(stage, k):
        for copy in edge_copies(stage, k):
            copy.start()

    def side_copies(stage, k):
        return (
            remote(
                hsend.at[stage, :, chunk(k), :],
                hrecv.at[stage, 0, :, chunk(k), :],
                hs_s.at[stage, 0, k],
                hs_r.at[stage, 0, k],
                gyp,
            ),
            remote(
                hsend.at[stage, :, chunk(k), :],
                hrecv.at[stage, 1, :, chunk(k), :],
                hs_s.at[stage, 1, k],
                hs_r.at[stage, 1, k],
                gym,
            ),
        )

    def send_sides(stage, k):
        for copy in side_copies(stage, k):
            copy.start()

    lane16 = lax.broadcasted_iota(jnp.int32, (lev, LANES), 1)
    level16 = lax.broadcasted_iota(jnp.int32, (lev, LANES), 0)
    depth16 = (level16 + c * lev).astype(jnp.float32)
    lane8 = lax.broadcasted_iota(jnp.int32, (GROUP, LANES), 1)
    level8 = lax.broadcasted_iota(jnp.int32, (GROUP, LANES), 0)

    def merged(ahead, behind, lanes):
        return jnp.where((lanes & 1) == 1, ahead, pltpu.roll(behind, 2, 1))

    def slot_of(both, m):
        return pltpu.roll(both, (126 - m) % LANES, 1)

    def packed(acc, x, m, lanes):
        return jnp.where((lanes >> 1) == (m >> 1), pltpu.roll(x, (m + 1) % LANES, 1), acc)

    def ahead_of(x, h, lanes):
        return jnp.where(lanes == LANES - 1, h, pltpu.roll(x, LANES - 1, 1))

    def behind_of(x, h, lanes):
        return jnp.where(lanes == 0, h, pltpu.roll(x, 1, 1))

    for f in range(4):
        pltpu.make_async_copy(fld.at[f, pl.ds(1, rows)], fld.at[f, pl.ds(1, rows)], lsem.at[f]).wait()
    acc = jnp.zeros((lev, LANES), jnp.float32)
    for r in range(rows):
        for f in range(4):
            acc = packed(acc, fld[f, r + 1], 8 * r + 2 * f, lane16)
    cps[...] = acc
    column_copies = (
        remote(cps, cpack.at[0], cs_s.at[0], cs_r.at[0], gyp),
        remote(cps, cpack.at[1], cs_s.at[1], cs_r.at[1], gym),
    )
    for copy in column_copies:
        copy.start()

    for i, ref in enumerate((mask_ref, bottom_ref)):
        pltpu.make_async_copy(ref, mb.at[i, pl.ds(1, rows)], lsem.at[4 + i]).wait()

    def reach(m, b):
        return jnp.where(m == 1, b, 0).astype(jnp.float32)

    def wet_row(e, valid):
        depth = reach(mb[0, e], mb[1, e])
        if valid is not None:
            depth = jnp.where(valid, depth, 0.0)
        w = jnp.where(depth16 < depth, 1.0, 0.0)
        d = w * (-0.2 * fld[2, e] + 0.8 * fld[3, e])
        wet[e] = w
        den[e] = d
        tot[c, e] = jnp.sum(d, axis=0, keepdims=True)

    def own_row(r, _):
        wet_row(r + 1, None)
        return 0

    lax.fori_loop(0, rows, own_row, 0)

    def pack_chunk(stage, src, k):
        for pair in range(sub // 2):
            a = jnp.zeros((GROUP, LANES), jnp.float32)
            for half in range(2):
                for t in range(ntr):
                    a = packed(a, src[t, 2 * pair + half, chunk(k), :], 64 * half + 2 * t, lane8)
            hsend[stage, pair, chunk(k), :] = a

    def pack_sides(k, _):
        pltpu.make_async_copy(
            q0.at[:, :, chunk(k), :], q0.at[:, :, chunk(k), :], lsem.at[6 + k]
        ).wait()
        pack_chunk(0, q0, k)
        return 0

    lax.fori_loop(0, nchunk, pack_sides, 0)

    for copy in first:
        copy.wait_recv()
    for copy in column_copies:
        copy.wait_recv()
    wet_row(0, g > 0)
    wet_row(rows + 1, g < ng - 1)
    both = merged(cpack[1], cpack[0], lane16)
    for r in range(rows):
        for f in range(4):
            fldh[f, r] = slot_of(both, 8 * r + 2 * f)

    def halo_columns(r, _):
        behind = jnp.broadcast_to(reach(mby[0, 0, r], mby[0, 1, r]), (lev, LANES))
        ahead = jnp.broadcast_to(reach(mby[1, 0, r], mby[1, 1, r]), (lev, LANES))
        behind = jnp.where(y > 0, pltpu.roll(behind, 1, 1), 0.0)
        ahead = jnp.where(y < ny - 1, pltpu.roll(ahead, LANES - 1, 1), 0.0)
        depth = jnp.where(lane16 == 0, behind, ahead)
        w = jnp.where(depth16 < depth, 1.0, 0.0)
        d = w * (-0.2 * fldh[2, r] + 0.8 * fldh[3, r])
        weth[r] = w
        denh[r] = d
        tot[c, rows + 2 + r] = jnp.sum(d, axis=0, keepdims=True)
        return 0

    lax.fori_loop(0, rows, halo_columns, 0)
    total_copies = [
        remote(tot.at[c], tot.at[c], ts_s.at[d], ts_r.at[d], peer) for d, peer in enumerate(peers)
    ]
    for copy in total_copies:
        copy.start()

    for d, peer in enumerate(peers):
        total_copies[d].wait_recv()

    def pressure_of(d, e):
        incl = d
        step = 1
        while step < lev:
            incl = incl + jnp.where(level16 >= step, pltpu.roll(incl, step, 0), 0.0)
            step *= 2
        offset = jnp.zeros((1, LANES), jnp.float32)
        for p in range(nc - 1):
            offset = offset + jnp.where(p < c, tot[p, e], 0.0)
        return offset + incl - 0.5 * d

    def pressure_row(e, _):
        prs[e] = pressure_of(den[e], e)
        return 0

    def pressure_column(r, _):
        prsh[r] = pressure_of(denh[r], rows + 2 + r)
        return 0

    lax.fori_loop(0, rows + 2, pressure_row, 0)
    lax.fori_loop(0, rows, pressure_column, 0)

    def east_row(e, _):
        v = (wet[e] * wet[e + 1]) * (
            fld[0, e] + DT_FLOW * (CORIOLIS * fld[1, e] - (prs[e + 1] - prs[e]))
        )
        vel[0, e] = v
        cour_e[e] = COURANT * jnp.tanh(v)
        return 0

    lax.fori_loop(0, rows + 1, east_row, 0)

    def north_group(p, _):
        pack = jnp.zeros((lev, LANES), jnp.float32)
        for i in range(sub):
            r = sub * p + i
            w, h, ps, ph = wet[r + 1], weth[r], prs[r + 1], prsh[r]
            v = (w * ahead_of(w, h, lane16)) * (
                fld[1, r + 1]
                + DT_FLOW * (-CORIOLIS * fld[0, r + 1] - (ahead_of(ps, ph, lane16) - ps))
            )
            vel[1, r + 1] = v
            cour_n[r] = COURANT * jnp.tanh(v)
            before = (w * h) * (
                fldh[1, r] + DT_FLOW * (-CORIOLIS * fldh[0, r] - (ps - ph))
            )
            pack = jnp.where(
                lane16 == i, jnp.broadcast_to(before[:, 0:1], (lev, LANES)), pack
            )
        cour_p[p] = COURANT * jnp.tanh(pack)
        return 0

    lax.fori_loop(0, nc, north_group, 0)

    mine = pl.ds(pl.multiple_of(c * lev, lev), lev)
    velocity_copies = []
    for d, peer in enumerate(peers):
        p = peer["comp"]
        for n, (src, dst) in enumerate(
            (
                (cour_e.at[pl.ds(sub * p, sub + 1)], cer.at[:, mine, :]),
                (cour_n.at[pl.ds(sub * p, sub)], cnr.at[:, mine, :]),
                (cour_p.at[p], cpr.at[mine, :]),
            )
        ):
            velocity_copies.append(remote(src, dst, as_s.at[d, n], as_r.at[d, n], peer))
    for copy in velocity_copies:
        copy.start()
    for k in range(DEPTH):
        send_sides(0, k)
        send_edges(0, k)
    for i in range(sub + 1):
        cer[i, mine, :] = cour_e[sub * c + i]
    for i in range(sub):
        cnr[i, mine, :] = cour_n[sub * c + i]
    cpr[mine, :] = cour_p[c]

    def mixing_row(r, _):
        w, h = wet[r + 1], weth[r]
        open_e, open_w = w * wet[r + 2], wet[r] * w
        open_n, open_s = w * ahead_of(w, h, lane16), w * behind_of(w, h, lane16)
        for i in range(2):
            x, xh = fld[2 + i, r + 1], fldh[2 + i, r]
            flux_e = open_e * (fld[2 + i, r + 2] - x)
            flux_w = open_w * (x - fld[2 + i, r])
            flux_n = open_n * (ahead_of(x, xh, lane16) - x)
            flux_s = open_s * (x - behind_of(x, xh, lane16))
            mixed[i, r] = x + MIXING * ((flux_e - flux_w) + (flux_n - flux_s))
        return 0

    lax.fori_loop(0, rows, mixing_row, 0)

    def store_rows(r, _):
        pltpu.make_async_copy(vel.at[0, r + 1], east_out.at[:, r, 0, :], osem.at[0]).start()
        pltpu.make_async_copy(vel.at[1, r + 1], north_out.at[:, r, 0, :], osem.at[1]).start()
        pltpu.make_async_copy(mixed.at[1, r], salt_out.at[:, r, 0, :], osem.at[2]).start()
        return 0

    lax.fori_loop(0, rows, store_rows, 0)

    for copy in velocity_copies:
        copy.wait_recv()

    def wet_chunk(k, r):
        depth = reach(mb[0, sub * c + r + 1], mb[1, sub * c + r + 1])
        return jnp.where((level8 + k * GROUP).astype(jnp.float32) < depth, 1.0, 0.0)

    def coefficients(k):
        for r in range(sub):
            ce, cw, cn = cer[r + 1, chunk(k), :], cer[r, chunk(k), :], cnr[r, chunk(k), :]
            edge = cpr[chunk(k), :]
            if r:
                edge = pltpu.roll(edge, LANES - r, 1)
            cs = behind_of(cn, edge, lane8)
            w = wet_chunk(k, r)
            out_e, in_e = jnp.maximum(ce, 0.0), jnp.minimum(ce, 0.0)
            out_w, in_w = jnp.maximum(cw, 0.0), jnp.minimum(cw, 0.0)
            out_n, in_n = jnp.maximum(cn, 0.0), jnp.minimum(cn, 0.0)
            out_s, in_s = jnp.maximum(cs, 0.0), jnp.minimum(cs, 0.0)
            wcol[r, chunk(k), :] = w
            coef[0, r, chunk(k), :] = w * (1.0 - (out_e - in_w) - (out_n - in_s))
            coef[1, r, chunk(k), :] = -w * in_e
            coef[2, r, chunk(k), :] = w * out_w
            coef[3, r, chunk(k), :] = -w * in_n
            coef[4, r, chunk(k), :] = w * out_s

    def substep(k, src, dst, stage, each):
        cf = [[coef[i, r, chunk(k), :] for i in range(5)] for r in range(sub)]
        both = [
            merged(hrecv[stage, 1, p, chunk(k), :], hrecv[stage, 0, p, chunk(k), :], lane8)
            for p in range(sub // 2)
        ]
        for t in range(ntr):
            q = [lo[stage, t, chunk(k), :]]
            q += [src[t, r, chunk(k), :] for r in range(sub)]
            q += [hi[stage, t, chunk(k), :]]
            for r in range(sub):
                x = q[r + 1]
                h = slot_of(both[r // 2], 64 * (r % 2) + 2 * t)
                new = (
                    cf[r][0] * x
                    + cf[r][1] * q[r + 2]
                    + cf[r][2] * q[r]
                    + cf[r][3] * ahead_of(x, h, lane8)
                    + cf[r][4] * behind_of(x, h, lane8)
                )
                dst[t, r, chunk(k), :] = new
                each(t, r, new)

    def first_substep(k):
        for copy in edge_copies(0, k):
            copy.wait_recv()
        for copy in side_copies(0, k):
            copy.wait_recv()
        coefficients(k)
        substep(k, q0, q1, 0, lambda t, r, new: None)
        send_edges(1, k)
        pack_chunk(1, q1, k)
        send_sides(1, k)

        @pl.when(k + DEPTH < nchunk)
        def _():
            send_sides(0, k + DEPTH)
            send_edges(0, k + DEPTH)


    for copy in settings:
        copy.wait()
    layer = 2.0 / levels
    block = 4
    carry[...] = jnp.zeros_like(carry)

    def second_substep(k):
        for copy in edge_copies(1, k):
            copy.wait_recv()
        for copy in side_copies(1, k):
            copy.wait_recv()
        optical = [jnp.zeros((GROUP, LANES), jnp.float32) for _ in range(sub)]

        def each(t, r, new):
            optical[r] = optical[r] + absorb_ref[t] * new

        substep(k, q1, q0, 1, each)
        light, scaled, nutrient = [], [], []
        for r in range(sub):
            step = layer * (CLEAR_WATER + optical[r])
            above = jnp.where(level8 >= 1, pltpu.roll(step, 1, 0), 0.0)
            for d in (1, 2, 4):
                above = above + jnp.where(level8 >= d, pltpu.roll(above, d, 0), 0.0)
            before = carry[r]
            carry[r] = before + jnp.sum(step, axis=0, keepdims=True)
            arriving = sun_ref[r] * jnp.exp(-(before + above))
            warm[r, chunk(k), :] = (
                wcol[r, chunk(k), :] * arriving * (1.0 - jnp.exp(-step)) / layer
            )
            light.append(arriving * jnp.exp(-0.5 * step))
            nutrient.append(q0[0, r, chunk(k), :])
            scaled.append(nutrient[r] * light[r])
        for t in range(ntr):
            for r in range(sub):
                below = (half_ref[t] + nutrient[r]) * (light[r] + light_half_ref[t])
                upt[t, r] = (growth_ref[t] * scaled[r]) * q0[t, r, chunk(k), :] / below
        half_wet = [DT_BIO * wcol[r, chunk(k), :] for r in range(sub)]

        def react(b, _):
            sums = [[jnp.zeros((GROUP, LANES), jnp.float32)] * sub for _ in range(block)]
            for t in range(ntr):
                u = [upt[t, r] for r in range(sub)]
                for i in range(block):
                    s = stoich_ref[block * b + i, t]
                    sums[i] = [sums[i][r] + s * u[r] for r in range(sub)]
            for i in range(block):
                for r in range(sub):
                    res[block * b + i, r, chunk(k), :] = (
                        q0[block * b + i, r, chunk(k), :] + half_wet[r] * sums[i][r]
                    )
            return 0

        lax.fori_loop(0, ntr // block, react, 0)
        for r in range(sub):
            pltpu.make_async_copy(
                res.at[:, r, chunk(k), :], result_out.at[:, chunk(k), r, 0, :], osem.at[3]
            ).start()

    def heat_copy(p):
        part = pl.ds(pl.multiple_of(p * lev, lev), lev)
        return remote(
            warm.at[:, part, :],
            heat.at[pl.ds(sub * c, sub)],
            ws_s.at[p],
            ws_r.at[c],
            {"comp": p, "gx": g, "gy": y},
        )

    def send_heat(p):
        @pl.when(p != c)
        def _():
            heat_copy(p).start()

        @pl.when(p == c)
        def _():
            part = pl.ds(pl.multiple_of(p * lev, lev), lev)
            for r in range(sub):
                heat[sub * c + r] = warm[r, part, :]

    each_peer = lev // GROUP

    def advance(k, _):
        @pl.when(k < nchunk)
        def _():
            first_substep(k)

        @pl.when(k > 0)
        def _():
            second_substep(k - 1)

        @pl.when((k > 0) & (lax.rem(k, each_peer) == 0))
        def _():
            send_heat(k // each_peer - 1)

        return 0

    lax.fori_loop(0, nchunk + 1, advance, 0)

    for d in range(1, nc):
        p = lax.rem(c + nc - d, nc)
        remote(
            warm.at[:, pl.ds(0, lev), :],
            heat.at[pl.ds(sub * p, sub)],
            ws_s.at[p],
            ws_r.at[p],
            {"comp": p, "gx": g, "gy": y},
        ).wait_recv()

    def final_row(r, _):
        warmed = mixed[0, r] + WARMING_FACTOR * heat[r]
        fin[0, r] = warmed
        fin[1, r] = wet[r + 1] * (0.2 * warmed - 0.8 * mixed[1, r])
        return 0

    lax.fori_loop(0, rows, final_row, 0)

    def store_final(r, _):
        pltpu.make_async_copy(fin.at[0, r], warmed_out.at[:, r, 0, :], osem.at[4]).start()
        pltpu.make_async_copy(fin.at[1, r], buoy_out.at[:, r, 0, :], osem.at[5]).start()
        return 0

    lax.fori_loop(0, rows, store_final, 0)

    for copy in first + list(column_copies) + total_copies + velocity_copies:
        copy.wait_send()

    def drain(k, _):
        for stage in range(2):
            for copy in edge_copies(stage, k) + side_copies(stage, k):
                copy.wait_send()
        return 0

    lax.fori_loop(0, nchunk, drain, 0)
    for d in range(1, nc):
        heat_copy(lax.rem(c + d, nc)).wait_send()
    for n, ref in enumerate(
        (vel.at[0, pl.ds(1, rows)], vel.at[1, pl.ds(1, rows)], mixed.at[1], res, fin.at[0], fin.at[1])
    ):
        pltpu.make_async_copy(ref, ref, osem.at[n]).wait()


def place_kernel(count, *refs):
    sources, targets = refs[:count], refs[count : 2 * count]
    held, sems = refs[2 * count : 3 * count], refs[3 * count]
    parts = 8
    copies = []
    for n in range(count):
        size = sources[n].shape[0] // parts
        for p in range(parts):
            part = pl.ds(p * size, size)
            copies.append(
                (
                    pltpu.make_async_copy(
                        sources[n].at[part], held[n].at[part], sems.at[0, n, p]
                    ),
                    pltpu.make_async_copy(
                        held[n].at[part], targets[n].at[part], sems.at[1, n, p]
                    ),
                )
            )
    copies = copies[(count - 1) * parts :] + copies[: (count - 1) * parts]
    for fetch, _ in copies:
        fetch.start()
    for fetch, put in copies:
        fetch.wait()
        put.start()
    for _, put in copies:
        put.wait()


def on_device(mesh_shape, *args):
    (
        zonal,
        merid,
        therm,
        brine,
        mask,
        bottom,
        tracers,
        sun,
        absorb,
        growth,
        half,
        light_half,
        stoich,
    ) = args
    lev, rows, lanes = zonal.shape
    ntr, levels, sub = tracers.shape[0], tracers.shape[1], tracers.shape[4]
    nc, ng, ny = mesh_shape
    nchunk = levels // GROUP
    f32, i32 = jnp.float32, jnp.int32
    column = (lev, rows, 1, lanes)
    vm, dma = pltpu.VMEM, pltpu.SemaphoreType.DMA
    anywhere = pl.BlockSpec(memory_space=pl.ANY)
    scratch = [
        vm((4, rows + 2, lev, lanes), f32),
        vm((4, rows, lev, lanes), f32),
        vm((2, rows + 2, 1, lanes), i32),
        vm((2, 2, rows, 1, lanes), i32),
        vm((rows + 2, lev, lanes), f32),
        vm((rows, lev, lanes), f32),
        vm((rows + 2, lev, lanes), f32),
        vm((rows, lev, lanes), f32),
        vm((nc, 2 * rows + 2, 1, lanes), f32),
        vm((rows + 2, lev, lanes), f32),
        vm((rows, lev, lanes), f32),
        vm((2, rows + 1, lev, lanes), f32),
        vm((rows + 1, lev, lanes), f32),
        vm((rows, lev, lanes), f32),
        vm((nc, lev, lanes), f32),
        vm((sub + 1, levels, lanes), f32),
        vm((sub, levels, lanes), f32),
        vm((levels, lanes), f32),
        vm((lev, lanes), f32),
        vm((2, lev, lanes), f32),
        vm((2, rows, lev, lanes), f32),
        vm((rows, lev, lanes), f32),
        vm((2, rows, lev, lanes), f32),
        vm((ntr, sub, levels, lanes), f32),
        vm((ntr, sub, levels, lanes), f32),
        vm((ntr, sub, levels, lanes), f32),
        vm((2, ntr, levels, lanes), f32),
        vm((2, ntr, levels, lanes), f32),
        vm((2, sub // 2, levels, lanes), f32),
        vm((2, 2, sub // 2, levels, lanes), f32),
        vm((5, sub, levels, lanes), f32),
        vm((sub, levels, lanes), f32),
        vm((sub, levels, lanes), f32),
        vm((sub, GROUP, lanes), f32),
        vm((ntr, sub, GROUP, lanes), f32),
        vm((sub, 1, lanes), f32),
        pltpu.SMEM((ntr,), f32),
        pltpu.SMEM((ntr,), f32),
        pltpu.SMEM((ntr,), f32),
        pltpu.SMEM((ntr,), f32),
        pltpu.SMEM((ntr, ntr), f32),
        dma((12 + nchunk,)),
        dma((6,)),
        dma((14,)),
        dma((14,)),
        dma((2,)),
        dma((2,)),
        dma((nc - 1,)),
        dma((nc - 1,)),
        dma((nc - 1, 3)),
        dma((nc - 1, 3)),
        dma((2, 2, nchunk)),
        dma((2, 2, nchunk)),
        dma((2, 2, nchunk)),
        dma((2, 2, nchunk)),
        dma((nc,)),
        dma((nc,)),
    ]
    outs = pl.pallas_call(
        functools.partial(ocean_kernel, (ntr, levels, rows, lev, sub, ng, ny)),
        out_shape=[jax.ShapeDtypeStruct(column, f32)] * 5
        + [jax.ShapeDtypeStruct((ntr, levels, sub, 1, lanes), f32)],
        in_specs=[anywhere] * 13,
        out_specs=[anywhere] * 6,
        scratch_shapes=scratch,
        compiler_params=pltpu.CompilerParams(
            collective_id=0, has_side_effects=True, vmem_limit_bytes=67043328
        ),
        name="ocean",
    )(
        *(x.reshape(column) for x in (zonal, merid, therm, brine)),
        mask.reshape(rows, 1, lanes),
        bottom.reshape(rows, 1, lanes),
        tracers.reshape(ntr, levels, sub, 1, lanes),
        sun.reshape(sub, 1, lanes),
        absorb,
        growth,
        half,
        light_half,
        stoich,
    )
    outs = [x.reshape(zonal.shape) for x in outs[:5]] + [outs[5].reshape(tracers.shape)]
    count = len(outs)
    return tuple(
        pl.pallas_call(
            functools.partial(place_kernel, count),
            out_shape=[jax.ShapeDtypeStruct(x.shape, f32) for x in outs],
            in_specs=[anywhere] * count,
            out_specs=[anywhere] * count,
            scratch_shapes=[vm(x.shape, f32) for x in outs] + [dma((2, count, 8))],
            compiler_params=pltpu.CompilerParams(vmem_limit_bytes=67043328),
            name="place",
        )(*outs)
    )


def solution(mesh):
    field = P("comp", "gx", "gy")
    tile = P("gx", "gy")
    tracer = P(None, None, "gx", "comp", None, "gy")
    shape = tuple(mesh.shape[a] for a in ("comp", "gx", "gy"))
    return jax.shard_map(
        functools.partial(on_device, shape),
        mesh=mesh,
        in_specs=(field,) * 4 + (tile,) * 2 + (tracer, P("gx", "comp", None, "gy")) + (P(),) * 5,
        out_specs=(field,) * 5 + (tracer,),
        check_vma=False,
    )
```

```python
import functools

import jax
import jax.numpy as jnp
from jax import lax
from jax.experimental import pallas as pl
from jax.experimental.pallas import tpu as pltpu
from jax.sharding import PartitionSpec as P

MESH = pl.DeviceIdType.MESH
LANES = 128
GROUP = 8
DEPTH = 3

DT_FLOW = 0.1
CORIOLIS = 0.3
MIXING = 0.15
COURANT = 0.24
DT_BIO = 0.5
WARMING_FACTOR = 0.5
CLEAR_WATER = 0.5


def ocean_kernel(
    dims,
    zonal_ref,
    merid_ref,
    therm_ref,
    brine_ref,
    mask_ref,
    bottom_ref,
    tracer_ref,
    sun_in,
    absorb_in,
    growth_in,
    half_in,
    light_half_in,
    stoich_in,
    east_out,
    north_out,
    warmed_out,
    salt_out,
    buoy_out,
    result_out,
    fld,
    fldh,
    mb,
    mby,
    wet,
    weth,
    den,
    denh,
    tot,
    toty,
    prs,
    prsh,
    vel,
    cour_e,
    cour_n,
    cour_p,
    cer,
    cnr,
    cpr,
    cps,
    cpack,
    mixed,
    heat,
    fin,
    q0,
    q1,
    res,
    lo,
    hi,
    hsend,
    hrecv,
    coef,
    wcol,
    warm,
    carry,
    upt,
    sun_ref,
    absorb_ref,
    growth_ref,
    half_ref,
    light_half_ref,
    stoich_ref,
    lsem,
    osem,
    p1s,
    p1r,
    cs_s,
    cs_r,
    ts_s,
    ts_r,
    as_s,
    as_r,
    qs_s,
    qs_r,
    hs_s,
    hs_r,
    ws_s,
    ws_r,
):
    ntr, levels, rows, lev, sub, ng, ny = dims
    nchunk = levels // GROUP
    nc = levels // lev
    c, g, y = lax.axis_index("comp"), lax.axis_index("gx"), lax.axis_index("gy")
    up = {
        "comp": lax.rem(c + 1, nc),
        "gx": jnp.where(c == nc - 1, lax.rem(g + 1, ng), g),
        "gy": y,
    }
    down = {
        "comp": lax.rem(c + nc - 1, nc),
        "gx": jnp.where(c == 0, lax.rem(g + ng - 1, ng), g),
        "gy": y,
    }
    gxp = {"comp": c, "gx": lax.rem(g + 1, ng), "gy": y}
    gxm = {"comp": c, "gx": lax.rem(g + ng - 1, ng), "gy": y}
    gyp = {"comp": c, "gx": g, "gy": lax.rem(y + 1, ny)}
    gym = {"comp": c, "gx": g, "gy": lax.rem(y + ny - 1, ny)}
    peers = [{"comp": lax.rem(c + d, nc), "gx": g, "gy": y} for d in range(1, nc)]

    def remote(src, dst, send, recv, device):
        return pltpu.make_async_remote_copy(
            src_ref=src,
            dst_ref=dst,
            send_sem=send,
            recv_sem=recv,
            device_id=device,
            device_id_type=MESH,
        )

    def chunk(k):
        return pl.ds(pl.multiple_of(k * GROUP, GROUP), GROUP)

    barrier = pltpu.get_barrier_semaphore()
    partners = [up, down, gxp, gxm, gyp, gym] + peers
    for peer in peers:
        p = peer["comp"]
        partners += [{**near, "comp": p} for near in (gxp, gxm, gyp, gym)]
    for device in partners:
        pl.semaphore_signal(barrier, inc=1, device_id=device, device_id_type=MESH)

    fields = (zonal_ref, merid_ref, therm_ref, brine_ref)

    def load_rows(r, _):
        for f, ref in enumerate(fields):
            pltpu.make_async_copy(ref.at[:, r, 0, :], fld.at[f, r + 1], lsem.at[f]).start()
        return 0

    lax.fori_loop(0, rows, load_rows, 0)
    for i, ref in enumerate((mask_ref, bottom_ref)):
        pltpu.make_async_copy(ref, mb.at[i, pl.ds(1, rows)], lsem.at[4 + i]).start()

    def load_tracers(k, _):
        for r in range(sub):
            pltpu.make_async_copy(
                tracer_ref.at[:, chunk(k), r, 0, :], q0.at[:, r, chunk(k), :], lsem.at[6 + k]
            ).start()
        return 0

    lax.fori_loop(0, nchunk, load_tracers, 0)
    settings = [
        pltpu.make_async_copy(src, dst, lsem.at[6 + nchunk + n])
        for n, (src, dst) in enumerate(
            (
                (sun_in, sun_ref),
                (absorb_in, absorb_ref),
                (growth_in, growth_ref),
                (half_in, half_ref),
                (light_half_in, light_half_ref),
                (stoich_in, stoich_ref),
            )
        )
    ]
    for copy in settings:
        copy.start()

    pl.semaphore_wait(barrier, len(partners))

    first = []
    for f, ref in enumerate(fields):
        first.append((ref.at[:, rows - 1, 0, :], fld.at[f, 0], gxp))
    for f in (2, 3):
        first.append((fields[f].at[:, 0, 0, :], fld.at[f, rows + 1], gxm))
    for i, ref in enumerate((mask_ref, bottom_ref)):
        first.append((ref.at[pl.ds(rows - 1, 1)], mb.at[i, pl.ds(0, 1)], gxp))
        first.append((ref.at[pl.ds(0, 1)], mb.at[i, pl.ds(rows + 1, 1)], gxm))
        first.append((ref, mby.at[0, i], gyp))
        first.append((ref, mby.at[1, i], gym))
    first = [
        remote(src, dst, p1s.at[n], p1r.at[n], device)
        for n, (src, dst, device) in enumerate(first)
    ]
    for copy in first:
        copy.start()

    def edge_copies(stage, k):
        if stage == 0:
            top = tracer_ref.at[:, chunk(k), sub - 1, 0, :]
            low = tracer_ref.at[:, chunk(k), 0, 0, :]
        else:
            top = q1.at[:, sub - 1, chunk(k), :]
            low = q1.at[:, 0, chunk(k), :]
        return (
            remote(
                top, lo.at[stage, :, chunk(k), :], qs_s.at[stage, 0, k], qs_r.at[stage, 0, k], up
            ),
            remote(
                low, hi.at[stage, :, chunk(k), :], qs_s.at[stage, 1, k], qs_r.at[stage, 1, k], down
            ),
        )

    def send_edges(stage, k):
        for copy in edge_copies(stage, k):
            copy.start()

    def side_copies(stage, k):
        return (
            remote(
                hsend.at[stage, :, chunk(k), :],
                hrecv.at[stage, 0, :, chunk(k), :],
                hs_s.at[stage, 0, k],
                hs_r.at[stage, 0, k],
                gyp,
            ),
            remote(
                hsend.at[stage, :, chunk(k), :],
                hrecv.at[stage, 1, :, chunk(k), :],
                hs_s.at[stage, 1, k],
                hs_r.at[stage, 1, k],
                gym,
            ),
        )

    def send_sides(stage, k):
        for copy in side_copies(stage, k):
            copy.start()

    for k in range(1):
        send_edges(0, k)

    lane16 = lax.broadcasted_iota(jnp.int32, (lev, LANES), 1)
    level16 = lax.broadcasted_iota(jnp.int32, (lev, LANES), 0)
    depth16 = (level16 + c * lev).astype(jnp.float32)
    lane8 = lax.broadcasted_iota(jnp.int32, (GROUP, LANES), 1)
    level8 = lax.broadcasted_iota(jnp.int32, (GROUP, LANES), 0)

    def merged(ahead, behind, lanes):
        return jnp.where((lanes & 1) == 1, ahead, pltpu.roll(behind, 2, 1))

    def slot_of(both, m):
        return pltpu.roll(both, (126 - m) % LANES, 1)

    def packed(acc, x, m, lanes):
        return jnp.where((lanes >> 1) == (m >> 1), pltpu.roll(x, (m + 1) % LANES, 1), acc)

    def ahead_of(x, h, lanes):
        return jnp.where(lanes == LANES - 1, h, pltpu.roll(x, LANES - 1, 1))

    def behind_of(x, h, lanes):
        return jnp.where(lanes == 0, h, pltpu.roll(x, 1, 1))

    for f in range(4):
        pltpu.make_async_copy(fld.at[f, pl.ds(1, rows)], fld.at[f, pl.ds(1, rows)], lsem.at[f]).wait()
    acc = jnp.zeros((lev, LANES), jnp.float32)
    for r in range(rows):
        for f in range(4):
            acc = packed(acc, fld[f, r + 1], 8 * r + 2 * f, lane16)
    cps[...] = acc
    column_copies = (
        remote(cps, cpack.at[0], cs_s.at[0], cs_r.at[0], gyp),
        remote(cps, cpack.at[1], cs_s.at[1], cs_r.at[1], gym),
    )
    for copy in column_copies:
        copy.start()

    for i, ref in enumerate((mask_ref, bottom_ref)):
        pltpu.make_async_copy(ref, mb.at[i, pl.ds(1, rows)], lsem.at[4 + i]).wait()

    def reach(m, b):
        return jnp.where(m == 1, b, 0).astype(jnp.float32)

    def wet_row(e, valid):
        depth = reach(mb[0, e], mb[1, e])
        if valid is not None:
            depth = jnp.where(valid, depth, 0.0)
        w = jnp.where(depth16 < depth, 1.0, 0.0)
        d = w * (-0.2 * fld[2, e] + 0.8 * fld[3, e])
        wet[e] = w
        den[e] = d
        tot[c, e] = jnp.sum(d, axis=0, keepdims=True)

    def own_row(r, _):
        wet_row(r + 1, None)
        return 0

    lax.fori_loop(0, rows, own_row, 0)

    def total_copies(source, p):
        whole = tot.at[source, pl.ds(1, rows)]
        sends = (
            (whole, whole, {"gx": g, "gy": y}),
            (tot.at[source, pl.ds(rows, 1)], tot.at[source, pl.ds(0, 1)], gxp),
            (tot.at[source, pl.ds(1, 1)], tot.at[source, pl.ds(rows + 1, 1)], gxm),
            (whole, toty.at[0, source], gyp),
            (whole, toty.at[1, source], gym),
        )
        return [
            remote(src, dst, ts_s.at[n, p], ts_r.at[n, source], {**device, "comp": p})
            for n, (src, dst, device) in enumerate(sends)
        ]

    for p in range(1, nc):

        @pl.when(p > c)
        def _(p=p):
            for copy in total_copies(c, p):
                copy.start()

    def pack_chunk(stage, src, k):
        for pair in range(sub // 2):
            a = jnp.zeros((GROUP, LANES), jnp.float32)
            for half in range(2):
                for t in range(ntr):
                    a = packed(a, src[t, 2 * pair + half, chunk(k), :], 64 * half + 2 * t, lane8)
            hsend[stage, pair, chunk(k), :] = a

    def pack_sides(k, _):
        pltpu.make_async_copy(
            q0.at[:, :, chunk(k), :], q0.at[:, :, chunk(k), :], lsem.at[6 + k]
        ).wait()
        pack_chunk(0, q0, k)
        return 0

    lax.fori_loop(0, nchunk, pack_sides, 0)

    for copy in first:
        copy.wait_recv()
    for copy in column_copies:
        copy.wait_recv()
    wet_row(0, g > 0)
    wet_row(rows + 1, g < ng - 1)
    both = merged(cpack[1], cpack[0], lane16)
    for r in range(rows):
        for f in range(4):
            fldh[f, r] = slot_of(both, 8 * r + 2 * f)

    def halo_columns(r, _):
        behind = jnp.broadcast_to(reach(mby[0, 0, r], mby[0, 1, r]), (lev, LANES))
        ahead = jnp.broadcast_to(reach(mby[1, 0, r], mby[1, 1, r]), (lev, LANES))
        behind = jnp.where(y > 0, pltpu.roll(behind, 1, 1), 0.0)
        ahead = jnp.where(y < ny - 1, pltpu.roll(ahead, LANES - 1, 1), 0.0)
        depth = jnp.where(lane16 == 0, behind, ahead)
        w = jnp.where(depth16 < depth, 1.0, 0.0)
        d = w * (-0.2 * fldh[2, r] + 0.8 * fldh[3, r])
        weth[r] = w
        denh[r] = d
        return 0

    lax.fori_loop(0, rows, halo_columns, 0)

    for p in range(nc - 1):

        @pl.when(p < c)
        def _(p=p):
            for copy in total_copies(p, p):
                copy.wait_recv()

    def running(d):
        incl = d
        step = 1
        while step < lev:
            incl = incl + jnp.where(level16 >= step, pltpu.roll(incl, step, 0), 0.0)
            step *= 2
        return incl - 0.5 * d

    def levels_above(totals):
        offset = jnp.zeros((1, LANES), jnp.float32)
        for p in range(nc - 1):
            offset = offset + jnp.where(p < c, totals(p), 0.0)
        return jnp.broadcast_to(offset, (lev, LANES))

    def pressure_row(e, _):
        prs[e] = levels_above(lambda p: tot[p, e]) + running(den[e])
        return 0

    def pressure_column(r, _):
        behind = pltpu.roll(levels_above(lambda p: toty[0, p, r]), 1, 1)
        ahead = pltpu.roll(levels_above(lambda p: toty[1, p, r]), LANES - 1, 1)
        prsh[r] = jnp.where(lane16 == 0, behind, ahead) + running(denh[r])
        return 0

    lax.fori_loop(0, rows + 2, pressure_row, 0)
    lax.fori_loop(0, rows, pressure_column, 0)

    def east_row(e, _):
        v = (wet[e] * wet[e + 1]) * (
            fld[0, e] + DT_FLOW * (CORIOLIS * fld[1, e] - (prs[e + 1] - prs[e]))
        )
        vel[0, e] = v
        cour_e[e] = COURANT * jnp.tanh(v)
        return 0

    lax.fori_loop(0, rows + 1, east_row, 0)

    def north_group(p, _):
        pack = jnp.zeros((lev, LANES), jnp.float32)
        for i in range(sub):
            r = sub * p + i
            w, h, ps, ph = wet[r + 1], weth[r], prs[r + 1], prsh[r]
            v = (w * ahead_of(w, h, lane16)) * (
                fld[1, r + 1]
                + DT_FLOW * (-CORIOLIS * fld[0, r + 1] - (ahead_of(ps, ph, lane16) - ps))
            )
            vel[1, r + 1] = v
            cour_n[r] = COURANT * jnp.tanh(v)
            before = (w * h) * (
                fldh[1, r] + DT_FLOW * (-CORIOLIS * fldh[0, r] - (ps - ph))
            )
            pack = jnp.where(
                lane16 == i, jnp.broadcast_to(before[:, 0:1], (lev, LANES)), pack
            )
        cour_p[p] = COURANT * jnp.tanh(pack)
        return 0

    lax.fori_loop(0, nc, north_group, 0)

    mine = pl.ds(pl.multiple_of(c * lev, lev), lev)
    velocity_copies = []
    for d, peer in enumerate(peers):
        p = peer["comp"]
        for n, (src, dst) in enumerate(
            (
                (cour_e.at[pl.ds(sub * p, sub + 1)], cer.at[:, mine, :]),
                (cour_n.at[pl.ds(sub * p, sub)], cnr.at[:, mine, :]),
                (cour_p.at[p], cpr.at[mine, :]),
            )
        ):
            velocity_copies.append(remote(src, dst, as_s.at[d, n], as_r.at[d, n], peer))
    for copy in velocity_copies:
        copy.start()
    for k in range(1):
        send_sides(0, k)
    for i in range(sub + 1):
        cer[i, mine, :] = cour_e[sub * c + i]
    for i in range(sub):
        cnr[i, mine, :] = cour_n[sub * c + i]
    cpr[mine, :] = cour_p[c]

    def mixing_row(r, _):
        w, h = wet[r + 1], weth[r]
        open_e, open_w = w * wet[r + 2], wet[r] * w
        open_n, open_s = w * ahead_of(w, h, lane16), w * behind_of(w, h, lane16)
        for i in range(2):
            x, xh = fld[2 + i, r + 1], fldh[2 + i, r]
            flux_e = open_e * (fld[2 + i, r + 2] - x)
            flux_w = open_w * (x - fld[2 + i, r])
            flux_n = open_n * (ahead_of(x, xh, lane16) - x)
            flux_s = open_s * (x - behind_of(x, xh, lane16))
            mixed[i, r] = x + MIXING * ((flux_e - flux_w) + (flux_n - flux_s))
        return 0

    lax.fori_loop(0, rows, mixing_row, 0)

    def store_rows(r, _):
        pltpu.make_async_copy(vel.at[0, r + 1], east_out.at[:, r, 0, :], osem.at[0]).start()
        pltpu.make_async_copy(vel.at[1, r + 1], north_out.at[:, r, 0, :], osem.at[1]).start()
        pltpu.make_async_copy(mixed.at[1, r], salt_out.at[:, r, 0, :], osem.at[2]).start()
        return 0

    lax.fori_loop(0, rows, store_rows, 0)

    for copy in velocity_copies:
        copy.wait_recv()
    for k in range(1, DEPTH):
        send_sides(0, k)
        send_edges(0, k)

    def wet_chunk(k, r):
        depth = reach(mb[0, sub * c + r + 1], mb[1, sub * c + r + 1])
        return jnp.where((level8 + k * GROUP).astype(jnp.float32) < depth, 1.0, 0.0)

    def coefficients(k):
        for r in range(sub):
            ce, cw, cn = cer[r + 1, chunk(k), :], cer[r, chunk(k), :], cnr[r, chunk(k), :]
            edge = cpr[chunk(k), :]
            if r:
                edge = pltpu.roll(edge, LANES - r, 1)
            cs = behind_of(cn, edge, lane8)
            w = wet_chunk(k, r)
            out_e, in_e = jnp.maximum(ce, 0.0), jnp.minimum(ce, 0.0)
            out_w, in_w = jnp.maximum(cw, 0.0), jnp.minimum(cw, 0.0)
            out_n, in_n = jnp.maximum(cn, 0.0), jnp.minimum(cn, 0.0)
            out_s, in_s = jnp.maximum(cs, 0.0), jnp.minimum(cs, 0.0)
            wcol[r, chunk(k), :] = w
            coef[0, r, chunk(k), :] = w * (1.0 - (out_e - in_w) - (out_n - in_s))
            coef[1, r, chunk(k), :] = -w * in_e
            coef[2, r, chunk(k), :] = w * out_w
            coef[3, r, chunk(k), :] = -w * in_n
            coef[4, r, chunk(k), :] = w * out_s

    def substep(k, src, dst, stage, each):
        cf = [[coef[i, r, chunk(k), :] for i in range(5)] for r in range(sub)]
        both = [
            merged(hrecv[stage, 1, p, chunk(k), :], hrecv[stage, 0, p, chunk(k), :], lane8)
            for p in range(sub // 2)
        ]
        for t in range(ntr):
            q = [lo[stage, t, chunk(k), :]]
            q += [src[t, r, chunk(k), :] for r in range(sub)]
            q += [hi[stage, t, chunk(k), :]]
            for r in range(sub):
                x = q[r + 1]
                h = slot_of(both[r // 2], 64 * (r % 2) + 2 * t)
                new = (
                    cf[r][0] * x
                    + cf[r][1] * q[r + 2]
                    + cf[r][2] * q[r]
                    + cf[r][3] * ahead_of(x, h, lane8)
                    + cf[r][4] * behind_of(x, h, lane8)
                )
                dst[t, r, chunk(k), :] = new
                each(t, r, new)

    def first_substep(k):
        for copy in edge_copies(0, k):
            copy.wait_recv()
        for copy in side_copies(0, k):
            copy.wait_recv()
        coefficients(k)
        substep(k, q0, q1, 0, lambda t, r, new: None)
        send_edges(1, k)
        pack_chunk(1, q1, k)
        send_sides(1, k)

        @pl.when(k + DEPTH < nchunk)
        def _():
            send_sides(0, k + DEPTH)
            send_edges(0, k + DEPTH)


    for copy in settings:
        copy.wait()
    layer = 2.0 / levels
    block = 4
    carry[...] = jnp.zeros_like(carry)

    def second_substep(k):
        for copy in edge_copies(1, k):
            copy.wait_recv()
        for copy in side_copies(1, k):
            copy.wait_recv()
        optical = [jnp.zeros((GROUP, LANES), jnp.float32) for _ in range(sub)]

        def each(t, r, new):
            optical[r] = optical[r] + absorb_ref[t] * new

        substep(k, q1, q0, 1, each)
        light, scaled, nutrient = [], [], []
        for r in range(sub):
            step = layer * (CLEAR_WATER + optical[r])
            above = jnp.where(level8 >= 1, pltpu.roll(step, 1, 0), 0.0)
            for d in (1, 2, 4):
                above = above + jnp.where(level8 >= d, pltpu.roll(above, d, 0), 0.0)
            before = carry[r]
            carry[r] = before + jnp.sum(step, axis=0, keepdims=True)
            arriving = sun_ref[r] * jnp.exp(-(before + above))
            warm[r, chunk(k), :] = (
                wcol[r, chunk(k), :] * arriving * (1.0 - jnp.exp(-step)) / layer
            )
            light.append(arriving * jnp.exp(-0.5 * step))
            nutrient.append(q0[0, r, chunk(k), :])
            scaled.append(nutrient[r] * light[r])
        for t in range(ntr):
            for r in range(sub):
                below = (half_ref[t] + nutrient[r]) * (light[r] + light_half_ref[t])
                upt[t, r] = (growth_ref[t] * scaled[r]) * q0[t, r, chunk(k), :] / below
        half_wet = [DT_BIO * wcol[r, chunk(k), :] for r in range(sub)]

        def react(b, _):
            sums = [[jnp.zeros((GROUP, LANES), jnp.float32)] * sub for _ in range(block)]
            for t in range(ntr):
                u = [upt[t, r] for r in range(sub)]
                for i in range(block):
                    s = stoich_ref[block * b + i, t]
                    sums[i] = [sums[i][r] + s * u[r] for r in range(sub)]
            for i in range(block):
                for r in range(sub):
                    res[block * b + i, r, chunk(k), :] = (
                        q0[block * b + i, r, chunk(k), :] + half_wet[r] * sums[i][r]
                    )
            return 0

        lax.fori_loop(0, ntr // block, react, 0)
        for r in range(sub):
            pltpu.make_async_copy(
                res.at[:, r, chunk(k), :], result_out.at[:, chunk(k), r, 0, :], osem.at[3]
            ).start()

    def heat_copy(p):
        part = pl.ds(pl.multiple_of(p * lev, lev), lev)
        return remote(
            warm.at[:, part, :],
            heat.at[pl.ds(sub * c, sub)],
            ws_s.at[p],
            ws_r.at[c],
            {"comp": p, "gx": g, "gy": y},
        )

    def send_heat(p):
        @pl.when(p != c)
        def _():
            heat_copy(p).start()

        @pl.when(p == c)
        def _():
            part = pl.ds(pl.multiple_of(p * lev, lev), lev)
            for r in range(sub):
                heat[sub * c + r] = warm[r, part, :]

    each_peer = lev // GROUP

    def advance(k, _):
        @pl.when(k < nchunk)
        def _():
            first_substep(k)

        @pl.when(k > 0)
        def _():
            second_substep(k - 1)

        @pl.when((k > 0) & (lax.rem(k, each_peer) == 0))
        def _():
            send_heat(k // each_peer - 1)

        return 0

    lax.fori_loop(0, nchunk + 1, advance, 0)

    for d in range(1, nc):
        p = lax.rem(c + nc - d, nc)
        remote(
            warm.at[:, pl.ds(0, lev), :],
            heat.at[pl.ds(sub * p, sub)],
            ws_s.at[p],
            ws_r.at[p],
            {"comp": p, "gx": g, "gy": y},
        ).wait_recv()

    def final_row(r, _):
        warmed = mixed[0, r] + WARMING_FACTOR * heat[r]
        fin[0, r] = warmed
        fin[1, r] = wet[r + 1] * (0.2 * warmed - 0.8 * mixed[1, r])
        return 0

    lax.fori_loop(0, rows, final_row, 0)

    def store_final(r, _):
        pltpu.make_async_copy(fin.at[0, r], warmed_out.at[:, r, 0, :], osem.at[4]).start()
        pltpu.make_async_copy(fin.at[1, r], buoy_out.at[:, r, 0, :], osem.at[5]).start()
        return 0

    lax.fori_loop(0, rows, store_final, 0)

    for copy in first + list(column_copies) + velocity_copies:
        copy.wait_send()
    for p in range(1, nc):

        @pl.when(p > c)
        def _(p=p):
            for copy in total_copies(c, p):
                copy.wait_send()

    def drain(k, _):
        for stage in range(2):
            for copy in edge_copies(stage, k) + side_copies(stage, k):
                copy.wait_send()
        return 0

    lax.fori_loop(0, nchunk, drain, 0)
    for d in range(1, nc):
        heat_copy(lax.rem(c + d, nc)).wait_send()
    for n, ref in enumerate(
        (vel.at[0, pl.ds(1, rows)], vel.at[1, pl.ds(1, rows)], mixed.at[1], res, fin.at[0], fin.at[1])
    ):
        pltpu.make_async_copy(ref, ref, osem.at[n]).wait()


def place_kernel(count, *refs):
    sources, targets = refs[:count], refs[count : 2 * count]
    held, sems = refs[2 * count : 3 * count], refs[3 * count]
    parts = 8
    copies = []
    for n in range(count):
        size = sources[n].shape[0] // parts
        for p in range(parts):
            part = pl.ds(p * size, size)
            copies.append(
                (
                    pltpu.make_async_copy(
                        sources[n].at[part], held[n].at[part], sems.at[0, n, p]
                    ),
                    pltpu.make_async_copy(
                        held[n].at[part], targets[n].at[part], sems.at[1, n, p]
                    ),
                )
            )
    copies = copies[(count - 1) * parts :] + copies[: (count - 1) * parts]
    for fetch, _ in copies:
        fetch.start()
    for fetch, put in copies:
        fetch.wait()
        put.start()
    for _, put in copies:
        put.wait()


def on_device(mesh_shape, *args):
    (
        zonal,
        merid,
        therm,
        brine,
        mask,
        bottom,
        tracers,
        sun,
        absorb,
        growth,
        half,
        light_half,
        stoich,
    ) = args
    lev, rows, lanes = zonal.shape
    ntr, levels, sub = tracers.shape[0], tracers.shape[1], tracers.shape[4]
    nc, ng, ny = mesh_shape
    nchunk = levels // GROUP
    f32, i32 = jnp.float32, jnp.int32
    column = (lev, rows, 1, lanes)
    vm, dma = pltpu.VMEM, pltpu.SemaphoreType.DMA
    anywhere = pl.BlockSpec(memory_space=pl.ANY)
    scratch = [
        vm((4, rows + 2, lev, lanes), f32),
        vm((4, rows, lev, lanes), f32),
        vm((2, rows + 2, 1, lanes), i32),
        vm((2, 2, rows, 1, lanes), i32),
        vm((rows + 2, lev, lanes), f32),
        vm((rows, lev, lanes), f32),
        vm((rows + 2, lev, lanes), f32),
        vm((rows, lev, lanes), f32),
        vm((nc, rows + 2, 1, lanes), f32),
        vm((2, nc, rows, 1, lanes), f32),
        vm((rows + 2, lev, lanes), f32),
        vm((rows, lev, lanes), f32),
        vm((2, rows + 1, lev, lanes), f32),
        vm((rows + 1, lev, lanes), f32),
        vm((rows, lev, lanes), f32),
        vm((nc, lev, lanes), f32),
        vm((sub + 1, levels, lanes), f32),
        vm((sub, levels, lanes), f32),
        vm((levels, lanes), f32),
        vm((lev, lanes), f32),
        vm((2, lev, lanes), f32),
        vm((2, rows, lev, lanes), f32),
        vm((rows, lev, lanes), f32),
        vm((2, rows, lev, lanes), f32),
        vm((ntr, sub, levels, lanes), f32),
        vm((ntr, sub, levels, lanes), f32),
        vm((ntr, sub, levels, lanes), f32),
        vm((2, ntr, levels, lanes), f32),
        vm((2, ntr, levels, lanes), f32),
        vm((2, sub // 2, levels, lanes), f32),
        vm((2, 2, sub // 2, levels, lanes), f32),
        vm((5, sub, levels, lanes), f32),
        vm((sub, levels, lanes), f32),
        vm((sub, levels, lanes), f32),
        vm((sub, GROUP, lanes), f32),
        vm((ntr, sub, GROUP, lanes), f32),
        vm((sub, 1, lanes), f32),
        pltpu.SMEM((ntr,), f32),
        pltpu.SMEM((ntr,), f32),
        pltpu.SMEM((ntr,), f32),
        pltpu.SMEM((ntr,), f32),
        pltpu.SMEM((ntr, ntr), f32),
        dma((12 + nchunk,)),
        dma((6,)),
        dma((14,)),
        dma((14,)),
        dma((2,)),
        dma((2,)),
        dma((5, nc)),
        dma((5, nc)),
        dma((nc - 1, 3)),
        dma((nc - 1, 3)),
        dma((2, 2, nchunk)),
        dma((2, 2, nchunk)),
        dma((2, 2, nchunk)),
        dma((2, 2, nchunk)),
        dma((nc,)),
        dma((nc,)),
    ]
    outs = pl.pallas_call(
        functools.partial(ocean_kernel, (ntr, levels, rows, lev, sub, ng, ny)),
        out_shape=[jax.ShapeDtypeStruct(column, f32)] * 5
        + [jax.ShapeDtypeStruct((ntr, levels, sub, 1, lanes), f32)],
        in_specs=[anywhere] * 13,
        out_specs=[anywhere] * 6,
        scratch_shapes=scratch,
        compiler_params=pltpu.CompilerParams(
            collective_id=0, has_side_effects=True, vmem_limit_bytes=67043328
        ),
        name="ocean",
    )(
        *(x.reshape(column) for x in (zonal, merid, therm, brine)),
        mask.reshape(rows, 1, lanes),
        bottom.reshape(rows, 1, lanes),
        tracers.reshape(ntr, levels, sub, 1, lanes),
        sun.reshape(sub, 1, lanes),
        absorb,
        growth,
        half,
        light_half,
        stoich,
    )
    outs = [x.reshape(zonal.shape) for x in outs[:5]] + [outs[5].reshape(tracers.shape)]
    count = len(outs)
    return tuple(
        pl.pallas_call(
            functools.partial(place_kernel, count),
            out_shape=[jax.ShapeDtypeStruct(x.shape, f32) for x in outs],
            in_specs=[anywhere] * count,
            out_specs=[anywhere] * count,
            scratch_shapes=[vm(x.shape, f32) for x in outs] + [dma((2, count, 8))],
            compiler_params=pltpu.CompilerParams(vmem_limit_bytes=67043328),
            name="place",
        )(*outs)
    )


def solution(mesh):
    field = P("comp", "gx", "gy")
    tile = P("gx", "gy")
    tracer = P(None, None, "gx", "comp", None, "gy")
    shape = tuple(mesh.shape[a] for a in ("comp", "gx", "gy"))
    return jax.shard_map(
        functools.partial(on_device, shape),
        mesh=mesh,
        in_specs=(field,) * 4 + (tile,) * 2 + (tracer, P("gx", "comp", None, "gy")) + (P(),) * 5,
        out_specs=(field,) * 5 + (tracer,),
        check_vma=False,
    )
```

```python
import functools

import jax
import jax.numpy as jnp
from jax import lax
from jax.experimental import pallas as pl
from jax.experimental.pallas import tpu as pltpu
from jax.sharding import PartitionSpec as P

MESH = pl.DeviceIdType.MESH
LANES = 128
GROUP = 8
DEPTH = 3

DT_FLOW = 0.1
CORIOLIS = 0.3
MIXING = 0.15
COURANT = 0.24
DT_BIO = 0.5
WARMING_FACTOR = 0.5
CLEAR_WATER = 0.5


def ocean_kernel(
    dims,
    zonal_ref,
    merid_ref,
    therm_ref,
    brine_ref,
    mask_ref,
    bottom_ref,
    tracer_ref,
    sun_in,
    absorb_in,
    growth_in,
    half_in,
    light_half_in,
    stoich_in,
    east_out,
    north_out,
    warmed_out,
    salt_out,
    buoy_out,
    result_out,
    fld,
    fldh,
    mb,
    mby,
    wet,
    weth,
    den,
    denh,
    tot,
    toty,
    prs,
    prsh,
    vel,
    cour_e,
    cour_n,
    cour_p,
    cer,
    cnr,
    cpr,
    cps,
    cpack,
    mixed,
    heat,
    fin,
    q0,
    q1,
    res,
    lo,
    hi,
    hsend,
    hrecv,
    coef,
    wcol,
    warm,
    carry,
    upt,
    sun_ref,
    absorb_ref,
    growth_ref,
    half_ref,
    light_half_ref,
    stoich_ref,
    lsem,
    osem,
    p1s,
    p1r,
    cs_s,
    cs_r,
    ts_s,
    ts_r,
    as_s,
    as_r,
    qs_s,
    qs_r,
    hs_s,
    hs_r,
    ws_s,
    ws_r,
):
    ntr, levels, rows, lev, sub, ng, ny = dims
    nchunk = levels // GROUP
    nc = levels // lev
    c, g, y = lax.axis_index("comp"), lax.axis_index("gx"), lax.axis_index("gy")
    up = {
        "comp": lax.rem(c + 1, nc),
        "gx": jnp.where(c == nc - 1, lax.rem(g + 1, ng), g),
        "gy": y,
    }
    down = {
        "comp": lax.rem(c + nc - 1, nc),
        "gx": jnp.where(c == 0, lax.rem(g + ng - 1, ng), g),
        "gy": y,
    }
    gxp = {"comp": c, "gx": lax.rem(g + 1, ng), "gy": y}
    gxm = {"comp": c, "gx": lax.rem(g + ng - 1, ng), "gy": y}
    gyp = {"comp": c, "gx": g, "gy": lax.rem(y + 1, ny)}
    gym = {"comp": c, "gx": g, "gy": lax.rem(y + ny - 1, ny)}
    peers = [{"comp": lax.rem(c + d, nc), "gx": g, "gy": y} for d in range(1, nc)]

    def remote(src, dst, send, recv, device):
        return pltpu.make_async_remote_copy(
            src_ref=src,
            dst_ref=dst,
            send_sem=send,
            recv_sem=recv,
            device_id=device,
            device_id_type=MESH,
        )

    def chunk(k):
        return pl.ds(pl.multiple_of(k * GROUP, GROUP), GROUP)

    barrier = pltpu.get_barrier_semaphore()
    partners = [up, down, gxp, gxm, gyp, gym] + peers
    for peer in peers:
        p = peer["comp"]
        partners += [{**near, "comp": p} for near in (gxp, gxm, gyp, gym)]
    for device in partners:
        pl.semaphore_signal(barrier, inc=1, device_id=device, device_id_type=MESH)

    fields = (zonal_ref, merid_ref, therm_ref, brine_ref)

    def load_rows(r, _):
        for f, ref in enumerate(fields):
            pltpu.make_async_copy(ref.at[:, r, 0, :], fld.at[f, r + 1], lsem.at[f]).start()
        return 0

    lax.fori_loop(0, rows, load_rows, 0)
    for i, ref in enumerate((mask_ref, bottom_ref)):
        pltpu.make_async_copy(ref, mb.at[i, pl.ds(1, rows)], lsem.at[4 + i]).start()

    def load_tracers(k, _):
        for r in range(sub):
            pltpu.make_async_copy(
                tracer_ref.at[:, chunk(k), r, 0, :], q0.at[:, r, chunk(k), :], lsem.at[6 + k]
            ).start()
        return 0

    lax.fori_loop(0, nchunk, load_tracers, 0)
    settings = [
        pltpu.make_async_copy(src, dst, lsem.at[6 + nchunk + n])
        for n, (src, dst) in enumerate(
            (
                (sun_in, sun_ref),
                (absorb_in, absorb_ref),
                (growth_in, growth_ref),
                (half_in, half_ref),
                (light_half_in, light_half_ref),
                (stoich_in, stoich_ref),
            )
        )
    ]
    for copy in settings:
        copy.start()

    pl.semaphore_wait(barrier, len(partners))

    first = []
    for f, ref in enumerate(fields):
        first.append((ref.at[:, rows - 1, 0, :], fld.at[f, 0], gxp))
    for f in (2, 3):
        first.append((fields[f].at[:, 0, 0, :], fld.at[f, rows + 1], gxm))
    for i, ref in enumerate((mask_ref, bottom_ref)):
        first.append((ref.at[pl.ds(rows - 1, 1)], mb.at[i, pl.ds(0, 1)], gxp))
        first.append((ref.at[pl.ds(0, 1)], mb.at[i, pl.ds(rows + 1, 1)], gxm))
        first.append((ref, mby.at[0, i], gyp))
        first.append((ref, mby.at[1, i], gym))
    first = [
        remote(src, dst, p1s.at[n], p1r.at[n], device)
        for n, (src, dst, device) in enumerate(first)
    ]
    for copy in first:
        copy.start()

    def edge_copies(stage, k):
        if stage == 0:
            top = tracer_ref.at[:, chunk(k), sub - 1, 0, :]
            low = tracer_ref.at[:, chunk(k), 0, 0, :]
        else:
            top = q1.at[:, sub - 1, chunk(k), :]
            low = q1.at[:, 0, chunk(k), :]
        return (
            remote(
                top, lo.at[stage, :, chunk(k), :], qs_s.at[stage, 0, k], qs_r.at[stage, 0, k], up
            ),
            remote(
                low, hi.at[stage, :, chunk(k), :], qs_s.at[stage, 1, k], qs_r.at[stage, 1, k], down
            ),
        )

    def send_edges(stage, k):
        for copy in edge_copies(stage, k):
            copy.start()

    def side_copies(stage, k):
        return (
            remote(
                hsend.at[stage, :, chunk(k), :],
                hrecv.at[stage, 0, :, chunk(k), :],
                hs_s.at[stage, 0, k],
                hs_r.at[stage, 0, k],
                gyp,
            ),
            remote(
                hsend.at[stage, :, chunk(k), :],
                hrecv.at[stage, 1, :, chunk(k), :],
                hs_s.at[stage, 1, k],
                hs_r.at[stage, 1, k],
                gym,
            ),
        )

    def send_sides(stage, k):
        for copy in side_copies(stage, k):
            copy.start()

    for k in range(1):
        send_edges(0, k)

    lane16 = lax.broadcasted_iota(jnp.int32, (lev, LANES), 1)
    level16 = lax.broadcasted_iota(jnp.int32, (lev, LANES), 0)
    depth16 = (level16 + c * lev).astype(jnp.float32)
    lane8 = lax.broadcasted_iota(jnp.int32, (GROUP, LANES), 1)
    level8 = lax.broadcasted_iota(jnp.int32, (GROUP, LANES), 0)

    def merged(ahead, behind, lanes):
        return jnp.where((lanes & 1) == 1, ahead, pltpu.roll(behind, 2, 1))

    def slot_of(both, m):
        return pltpu.roll(both, (126 - m) % LANES, 1)

    def packed(acc, x, m, lanes):
        return jnp.where((lanes >> 1) == (m >> 1), pltpu.roll(x, (m + 1) % LANES, 1), acc)

    def ahead_of(x, h, lanes):
        return jnp.where(lanes == LANES - 1, h, pltpu.roll(x, LANES - 1, 1))

    def behind_of(x, h, lanes):
        return jnp.where(lanes == 0, h, pltpu.roll(x, 1, 1))

    for f in range(4):
        pltpu.make_async_copy(fld.at[f, pl.ds(1, rows)], fld.at[f, pl.ds(1, rows)], lsem.at[f]).wait()
    acc = jnp.zeros((lev, LANES), jnp.float32)
    for r in range(rows):
        for f in range(4):
            acc = packed(acc, fld[f, r + 1], 8 * r + 2 * f, lane16)
    cps[...] = acc
    column_copies = (
        remote(cps, cpack.at[0], cs_s.at[0], cs_r.at[0], gyp),
        remote(cps, cpack.at[1], cs_s.at[1], cs_r.at[1], gym),
    )
    for copy in column_copies:
        copy.start()

    for i, ref in enumerate((mask_ref, bottom_ref)):
        pltpu.make_async_copy(ref, mb.at[i, pl.ds(1, rows)], lsem.at[4 + i]).wait()

    def reach(m, b):
        return jnp.where(m == 1, b, 0).astype(jnp.float32)

    def wet_row(e, valid):
        depth = reach(mb[0, e], mb[1, e])
        if valid is not None:
            depth = jnp.where(valid, depth, 0.0)
        w = jnp.where(depth16 < depth, 1.0, 0.0)
        d = w * (-0.2 * fld[2, e] + 0.8 * fld[3, e])
        wet[e] = w
        den[e] = d
        tot[c, e] = jnp.sum(d, axis=0, keepdims=True)

    def own_row(r, _):
        wet_row(r + 1, None)
        return 0

    lax.fori_loop(0, rows, own_row, 0)

    def total_copies(source, p):
        whole = tot.at[source, pl.ds(1, rows)]
        sends = (
            (whole, whole, {"gx": g, "gy": y}),
            (tot.at[source, pl.ds(rows, 1)], tot.at[source, pl.ds(0, 1)], gxp),
            (tot.at[source, pl.ds(1, 1)], tot.at[source, pl.ds(rows + 1, 1)], gxm),
            (whole, toty.at[0, source], gyp),
            (whole, toty.at[1, source], gym),
        )
        return [
            remote(src, dst, ts_s.at[n, p], ts_r.at[n, source], {**device, "comp": p})
            for n, (src, dst, device) in enumerate(sends)
        ]

    for p in range(1, nc):

        @pl.when(p > c)
        def _(p=p):
            for copy in total_copies(c, p):
                copy.start()

    def pack_chunk(stage, src, k):
        for pair in range(sub // 2):
            a = jnp.zeros((GROUP, LANES), jnp.float32)
            for half in range(2):
                for t in range(ntr):
                    a = packed(a, src[t, 2 * pair + half, chunk(k), :], 64 * half + 2 * t, lane8)
            hsend[stage, pair, chunk(k), :] = a

    def pack_sides(k, _):
        pltpu.make_async_copy(
            q0.at[:, :, chunk(k), :], q0.at[:, :, chunk(k), :], lsem.at[6 + k]
        ).wait()
        pack_chunk(0, q0, k)
        return 0

    lax.fori_loop(0, nchunk, pack_sides, 0)

    for copy in first:
        copy.wait_recv()
    for copy in column_copies:
        copy.wait_recv()
    wet_row(0, g > 0)
    wet_row(rows + 1, g < ng - 1)
    both = merged(cpack[1], cpack[0], lane16)
    for r in range(rows):
        for f in range(4):
            fldh[f, r] = slot_of(both, 8 * r + 2 * f)

    def halo_columns(r, _):
        behind = jnp.broadcast_to(reach(mby[0, 0, r], mby[0, 1, r]), (lev, LANES))
        ahead = jnp.broadcast_to(reach(mby[1, 0, r], mby[1, 1, r]), (lev, LANES))
        behind = jnp.where(y > 0, pltpu.roll(behind, 1, 1), 0.0)
        ahead = jnp.where(y < ny - 1, pltpu.roll(ahead, LANES - 1, 1), 0.0)
        depth = jnp.where(lane16 == 0, behind, ahead)
        w = jnp.where(depth16 < depth, 1.0, 0.0)
        d = w * (-0.2 * fldh[2, r] + 0.8 * fldh[3, r])
        weth[r] = w
        denh[r] = d
        return 0

    lax.fori_loop(0, rows, halo_columns, 0)

    for k in range(1, 2):
        send_edges(0, k)

    for p in range(nc - 1):

        @pl.when(p < c)
        def _(p=p):
            for copy in total_copies(p, p):
                copy.wait_recv()

    def running(d):
        incl = d
        step = 1
        while step < lev:
            incl = incl + jnp.where(level16 >= step, pltpu.roll(incl, step, 0), 0.0)
            step *= 2
        return incl - 0.5 * d

    def levels_above(totals):
        offset = jnp.zeros((1, LANES), jnp.float32)
        for p in range(nc - 1):
            offset = offset + jnp.where(p < c, totals(p), 0.0)
        return jnp.broadcast_to(offset, (lev, LANES))

    def pressure_row(e, _):
        prs[e] = levels_above(lambda p: tot[p, e]) + running(den[e])
        return 0

    def pressure_column(r, _):
        behind = pltpu.roll(levels_above(lambda p: toty[0, p, r]), 1, 1)
        ahead = pltpu.roll(levels_above(lambda p: toty[1, p, r]), LANES - 1, 1)
        prsh[r] = jnp.where(lane16 == 0, behind, ahead) + running(denh[r])
        return 0

    lax.fori_loop(0, rows + 2, pressure_row, 0)
    lax.fori_loop(0, rows, pressure_column, 0)

    def east_row(e, _):
        v = (wet[e] * wet[e + 1]) * (
            fld[0, e] + DT_FLOW * (CORIOLIS * fld[1, e] - (prs[e + 1] - prs[e]))
        )
        vel[0, e] = v
        cour_e[e] = COURANT * jnp.tanh(v)
        return 0

    lax.fori_loop(0, rows + 1, east_row, 0)

    def north_group(p, _):
        pack = jnp.zeros((lev, LANES), jnp.float32)
        for i in range(sub):
            r = sub * p + i
            w, h, ps, ph = wet[r + 1], weth[r], prs[r + 1], prsh[r]
            v = (w * ahead_of(w, h, lane16)) * (
                fld[1, r + 1]
                + DT_FLOW * (-CORIOLIS * fld[0, r + 1] - (ahead_of(ps, ph, lane16) - ps))
            )
            vel[1, r + 1] = v
            cour_n[r] = COURANT * jnp.tanh(v)
            before = (w * h) * (
                fldh[1, r] + DT_FLOW * (-CORIOLIS * fldh[0, r] - (ps - ph))
            )
            pack = jnp.where(
                lane16 == i, jnp.broadcast_to(before[:, 0:1], (lev, LANES)), pack
            )
        cour_p[p] = COURANT * jnp.tanh(pack)
        return 0

    lax.fori_loop(0, nc, north_group, 0)

    mine = pl.ds(pl.multiple_of(c * lev, lev), lev)
    velocity_copies = []
    for d, peer in enumerate(peers):
        p = peer["comp"]
        for n, (src, dst) in enumerate(
            (
                (cour_e.at[pl.ds(sub * p, sub + 1)], cer.at[:, mine, :]),
                (cour_n.at[pl.ds(sub * p, sub)], cnr.at[:, mine, :]),
                (cour_p.at[p], cpr.at[mine, :]),
            )
        ):
            velocity_copies.append(remote(src, dst, as_s.at[d, n], as_r.at[d, n], peer))
    for copy in velocity_copies:
        copy.start()
    for k in range(2):
        send_sides(0, k)
    for i in range(sub + 1):
        cer[i, mine, :] = cour_e[sub * c + i]
    for i in range(sub):
        cnr[i, mine, :] = cour_n[sub * c + i]
    cpr[mine, :] = cour_p[c]

    def mixing_row(r, _):
        w, h = wet[r + 1], weth[r]
        open_e, open_w = w * wet[r + 2], wet[r] * w
        open_n, open_s = w * ahead_of(w, h, lane16), w * behind_of(w, h, lane16)
        for i in range(2):
            x, xh = fld[2 + i, r + 1], fldh[2 + i, r]
            flux_e = open_e * (fld[2 + i, r + 2] - x)
            flux_w = open_w * (x - fld[2 + i, r])
            flux_n = open_n * (ahead_of(x, xh, lane16) - x)
            flux_s = open_s * (x - behind_of(x, xh, lane16))
            mixed[i, r] = x + MIXING * ((flux_e - flux_w) + (flux_n - flux_s))
        return 0

    lax.fori_loop(0, rows, mixing_row, 0)

    def store_rows(r, _):
        pltpu.make_async_copy(vel.at[0, r + 1], east_out.at[:, r, 0, :], osem.at[0]).start()
        pltpu.make_async_copy(vel.at[1, r + 1], north_out.at[:, r, 0, :], osem.at[1]).start()
        pltpu.make_async_copy(mixed.at[1, r], salt_out.at[:, r, 0, :], osem.at[2]).start()
        return 0

    lax.fori_loop(0, rows, store_rows, 0)

    for copy in velocity_copies:
        copy.wait_recv()
    for k in range(2, DEPTH):
        send_sides(0, k)
        send_edges(0, k)

    def wet_chunk(k, r):
        depth = reach(mb[0, sub * c + r + 1], mb[1, sub * c + r + 1])
        return jnp.where((level8 + k * GROUP).astype(jnp.float32) < depth, 1.0, 0.0)

    def coefficients(k):
        for r in range(sub):
            ce, cw, cn = cer[r + 1, chunk(k), :], cer[r, chunk(k), :], cnr[r, chunk(k), :]
            edge = cpr[chunk(k), :]
            if r:
                edge = pltpu.roll(edge, LANES - r, 1)
            cs = behind_of(cn, edge, lane8)
            w = wet_chunk(k, r)
            out_e, in_e = jnp.maximum(ce, 0.0), jnp.minimum(ce, 0.0)
            out_w, in_w = jnp.maximum(cw, 0.0), jnp.minimum(cw, 0.0)
            out_n, in_n = jnp.maximum(cn, 0.0), jnp.minimum(cn, 0.0)
            out_s, in_s = jnp.maximum(cs, 0.0), jnp.minimum(cs, 0.0)
            wcol[r, chunk(k), :] = w
            coef[0, r, chunk(k), :] = w * (1.0 - (out_e - in_w) - (out_n - in_s))
            coef[1, r, chunk(k), :] = -w * in_e
            coef[2, r, chunk(k), :] = w * out_w
            coef[3, r, chunk(k), :] = -w * in_n
            coef[4, r, chunk(k), :] = w * out_s

    def substep(k, src, dst, stage, each):
        cf = [[coef[i, r, chunk(k), :] for i in range(5)] for r in range(sub)]
        both = [
            merged(hrecv[stage, 1, p, chunk(k), :], hrecv[stage, 0, p, chunk(k), :], lane8)
            for p in range(sub // 2)
        ]
        for t in range(ntr):
            q = [lo[stage, t, chunk(k), :]]
            q += [src[t, r, chunk(k), :] for r in range(sub)]
            q += [hi[stage, t, chunk(k), :]]
            for r in range(sub):
                x = q[r + 1]
                h = slot_of(both[r // 2], 64 * (r % 2) + 2 * t)
                new = (
                    cf[r][0] * x
                    + cf[r][1] * q[r + 2]
                    + cf[r][2] * q[r]
                    + cf[r][3] * ahead_of(x, h, lane8)
                    + cf[r][4] * behind_of(x, h, lane8)
                )
                dst[t, r, chunk(k), :] = new
                each(t, r, new)

    def first_substep(k):
        for copy in edge_copies(0, k):
            copy.wait_recv()
        for copy in side_copies(0, k):
            copy.wait_recv()
        coefficients(k)
        substep(k, q0, q1, 0, lambda t, r, new: None)
        send_edges(1, k)
        pack_chunk(1, q1, k)
        send_sides(1, k)

        @pl.when(k + DEPTH < nchunk)
        def _():
            send_sides(0, k + DEPTH)
            send_edges(0, k + DEPTH)


    for copy in settings:
        copy.wait()
    layer = 2.0 / levels
    block = 4
    carry[...] = jnp.zeros_like(carry)

    def second_substep(k):
        for copy in edge_copies(1, k):
            copy.wait_recv()
        for copy in side_copies(1, k):
            copy.wait_recv()
        optical = [jnp.zeros((GROUP, LANES), jnp.float32) for _ in range(sub)]

        def each(t, r, new):
            optical[r] = optical[r] + absorb_ref[t] * new

        substep(k, q1, q0, 1, each)
        light, scaled, nutrient = [], [], []
        for r in range(sub):
            step = layer * (CLEAR_WATER + optical[r])
            above = jnp.where(level8 >= 1, pltpu.roll(step, 1, 0), 0.0)
            for d in (1, 2, 4):
                above = above + jnp.where(level8 >= d, pltpu.roll(above, d, 0), 0.0)
            before = carry[r]
            carry[r] = before + jnp.sum(step, axis=0, keepdims=True)
            arriving = sun_ref[r] * jnp.exp(-(before + above))
            warm[r, chunk(k), :] = (
                wcol[r, chunk(k), :] * arriving * (1.0 - jnp.exp(-step)) / layer
            )
            light.append(arriving * jnp.exp(-0.5 * step))
            nutrient.append(q0[0, r, chunk(k), :])
            scaled.append(nutrient[r] * light[r])
        for t in range(ntr):
            for r in range(sub):
                below = (half_ref[t] + nutrient[r]) * (light[r] + light_half_ref[t])
                upt[t, r] = (growth_ref[t] * scaled[r]) * q0[t, r, chunk(k), :] / below
        half_wet = [DT_BIO * wcol[r, chunk(k), :] for r in range(sub)]

        def react(b, _):
            sums = [[jnp.zeros((GROUP, LANES), jnp.float32)] * sub for _ in range(block)]
            for t in range(ntr):
                u = [upt[t, r] for r in range(sub)]
                for i in range(block):
                    s = stoich_ref[block * b + i, t]
                    sums[i] = [sums[i][r] + s * u[r] for r in range(sub)]
            for i in range(block):
                for r in range(sub):
                    res[block * b + i, r, chunk(k), :] = (
                        q0[block * b + i, r, chunk(k), :] + half_wet[r] * sums[i][r]
                    )
            return 0

        lax.fori_loop(0, ntr // block, react, 0)
        for r in range(sub):
            pltpu.make_async_copy(
                res.at[:, r, chunk(k), :], result_out.at[:, chunk(k), r, 0, :], osem.at[3]
            ).start()

    def heat_copy(p):
        part = pl.ds(pl.multiple_of(p * lev, lev), lev)
        return remote(
            warm.at[:, part, :],
            heat.at[pl.ds(sub * c, sub)],
            ws_s.at[p],
            ws_r.at[c],
            {"comp": p, "gx": g, "gy": y},
        )

    def send_heat(p):
        @pl.when(p != c)
        def _():
            heat_copy(p).start()

        @pl.when(p == c)
        def _():
            part = pl.ds(pl.multiple_of(p * lev, lev), lev)
            for r in range(sub):
                heat[sub * c + r] = warm[r, part, :]

    each_peer = lev // GROUP

    def advance(k, _):
        @pl.when(k < nchunk)
        def _():
            first_substep(k)

        @pl.when(k > 0)
        def _():
            second_substep(k - 1)

        @pl.when((k > 0) & (lax.rem(k, each_peer) == 0))
        def _():
            send_heat(k // each_peer - 1)

        return 0

    lax.fori_loop(0, nchunk + 1, advance, 0)

    for d in range(1, nc):
        p = lax.rem(c + nc - d, nc)
        remote(
            warm.at[:, pl.ds(0, lev), :],
            heat.at[pl.ds(sub * p, sub)],
            ws_s.at[p],
            ws_r.at[p],
            {"comp": p, "gx": g, "gy": y},
        ).wait_recv()

    def final_row(r, _):
        warmed = mixed[0, r] + WARMING_FACTOR * heat[r]
        fin[0, r] = warmed
        fin[1, r] = wet[r + 1] * (0.2 * warmed - 0.8 * mixed[1, r])
        return 0

    lax.fori_loop(0, rows, final_row, 0)

    def store_final(r, _):
        pltpu.make_async_copy(fin.at[0, r], warmed_out.at[:, r, 0, :], osem.at[4]).start()
        pltpu.make_async_copy(fin.at[1, r], buoy_out.at[:, r, 0, :], osem.at[5]).start()
        return 0

    lax.fori_loop(0, rows, store_final, 0)

    for copy in first + list(column_copies) + velocity_copies:
        copy.wait_send()
    for p in range(1, nc):

        @pl.when(p > c)
        def _(p=p):
            for copy in total_copies(c, p):
                copy.wait_send()

    def drain(k, _):
        for stage in range(2):
            for copy in edge_copies(stage, k) + side_copies(stage, k):
                copy.wait_send()
        return 0

    lax.fori_loop(0, nchunk, drain, 0)
    for d in range(1, nc):
        heat_copy(lax.rem(c + d, nc)).wait_send()
    for n, ref in enumerate(
        (vel.at[0, pl.ds(1, rows)], vel.at[1, pl.ds(1, rows)], mixed.at[1], res, fin.at[0], fin.at[1])
    ):
        pltpu.make_async_copy(ref, ref, osem.at[n]).wait()


def place_kernel(count, *refs):
    sources, targets = refs[:count], refs[count : 2 * count]
    held, sems = refs[2 * count : 3 * count], refs[3 * count]
    parts = 8
    copies = []
    for n in range(count):
        size = sources[n].shape[0] // parts
        for p in range(parts):
            part = pl.ds(p * size, size)
            copies.append(
                (
                    pltpu.make_async_copy(
                        sources[n].at[part], held[n].at[part], sems.at[0, n, p]
                    ),
                    pltpu.make_async_copy(
                        held[n].at[part], targets[n].at[part], sems.at[1, n, p]
                    ),
                )
            )
    copies = copies[(count - 1) * parts :] + copies[: (count - 1) * parts]
    for fetch, _ in copies:
        fetch.start()
    for fetch, put in copies:
        fetch.wait()
        put.start()
    for _, put in copies:
        put.wait()


def on_device(mesh_shape, *args):
    (
        zonal,
        merid,
        therm,
        brine,
        mask,
        bottom,
        tracers,
        sun,
        absorb,
        growth,
        half,
        light_half,
        stoich,
    ) = args
    lev, rows, lanes = zonal.shape
    ntr, levels, sub = tracers.shape[0], tracers.shape[1], tracers.shape[4]
    nc, ng, ny = mesh_shape
    nchunk = levels // GROUP
    f32, i32 = jnp.float32, jnp.int32
    column = (lev, rows, 1, lanes)
    vm, dma = pltpu.VMEM, pltpu.SemaphoreType.DMA
    anywhere = pl.BlockSpec(memory_space=pl.ANY)
    scratch = [
        vm((4, rows + 2, lev, lanes), f32),
        vm((4, rows, lev, lanes), f32),
        vm((2, rows + 2, 1, lanes), i32),
        vm((2, 2, rows, 1, lanes), i32),
        vm((rows + 2, lev, lanes), f32),
        vm((rows, lev, lanes), f32),
        vm((rows + 2, lev, lanes), f32),
        vm((rows, lev, lanes), f32),
        vm((nc, rows + 2, 1, lanes), f32),
        vm((2, nc, rows, 1, lanes), f32),
        vm((rows + 2, lev, lanes), f32),
        vm((rows, lev, lanes), f32),
        vm((2, rows + 1, lev, lanes), f32),
        vm((rows + 1, lev, lanes), f32),
        vm((rows, lev, lanes), f32),
        vm((nc, lev, lanes), f32),
        vm((sub + 1, levels, lanes), f32),
        vm((sub, levels, lanes), f32),
        vm((levels, lanes), f32),
        vm((lev, lanes), f32),
        vm((2, lev, lanes), f32),
        vm((2, rows, lev, lanes), f32),
        vm((rows, lev, lanes), f32),
        vm((2, rows, lev, lanes), f32),
        vm((ntr, sub, levels, lanes), f32),
        vm((ntr, sub, levels, lanes), f32),
        vm((ntr, sub, levels, lanes), f32),
        vm((2, ntr, levels, lanes), f32),
        vm((2, ntr, levels, lanes), f32),
        vm((2, sub // 2, levels, lanes), f32),
        vm((2, 2, sub // 2, levels, lanes), f32),
        vm((5, sub, levels, lanes), f32),
        vm((sub, levels, lanes), f32),
        vm((sub, levels, lanes), f32),
        vm((sub, GROUP, lanes), f32),
        vm((ntr, sub, GROUP, lanes), f32),
        vm((sub, 1, lanes), f32),
        pltpu.SMEM((ntr,), f32),
        pltpu.SMEM((ntr,), f32),
        pltpu.SMEM((ntr,), f32),
        pltpu.SMEM((ntr,), f32),
        pltpu.SMEM((ntr, ntr), f32),
        dma((12 + nchunk,)),
        dma((6,)),
        dma((14,)),
        dma((14,)),
        dma((2,)),
        dma((2,)),
        dma((5, nc)),
        dma((5, nc)),
        dma((nc - 1, 3)),
        dma((nc - 1, 3)),
        dma((2, 2, nchunk)),
        dma((2, 2, nchunk)),
        dma((2, 2, nchunk)),
        dma((2, 2, nchunk)),
        dma((nc,)),
        dma((nc,)),
    ]
    outs = pl.pallas_call(
        functools.partial(ocean_kernel, (ntr, levels, rows, lev, sub, ng, ny)),
        out_shape=[jax.ShapeDtypeStruct(column, f32)] * 5
        + [jax.ShapeDtypeStruct((ntr, levels, sub, 1, lanes), f32)],
        in_specs=[anywhere] * 13,
        out_specs=[anywhere] * 6,
        scratch_shapes=scratch,
        compiler_params=pltpu.CompilerParams(
            collective_id=0, has_side_effects=True, vmem_limit_bytes=67043328
        ),
        name="ocean",
    )(
        *(x.reshape(column) for x in (zonal, merid, therm, brine)),
        mask.reshape(rows, 1, lanes),
        bottom.reshape(rows, 1, lanes),
        tracers.reshape(ntr, levels, sub, 1, lanes),
        sun.reshape(sub, 1, lanes),
        absorb,
        growth,
        half,
        light_half,
        stoich,
    )
    outs = [x.reshape(zonal.shape) for x in outs[:5]] + [outs[5].reshape(tracers.shape)]
    count = len(outs)
    return tuple(
        pl.pallas_call(
            functools.partial(place_kernel, count),
            out_shape=[jax.ShapeDtypeStruct(x.shape, f32) for x in outs],
            in_specs=[anywhere] * count,
            out_specs=[anywhere] * count,
            scratch_shapes=[vm(x.shape, f32) for x in outs] + [dma((2, count, 8))],
            compiler_params=pltpu.CompilerParams(vmem_limit_bytes=67043328),
            name="place",
        )(*outs)
    )


def solution(mesh):
    field = P("comp", "gx", "gy")
    tile = P("gx", "gy")
    tracer = P(None, None, "gx", "comp", None, "gy")
    shape = tuple(mesh.shape[a] for a in ("comp", "gx", "gy"))
    return jax.shard_map(
        functools.partial(on_device, shape),
        mesh=mesh,
        in_specs=(field,) * 4 + (tile,) * 2 + (tracer, P("gx", "comp", None, "gy")) + (P(),) * 5,
        out_specs=(field,) * 5 + (tracer,),
        check_vma=False,
    )
```

```python
import functools

import jax
import jax.numpy as jnp
from jax import lax
from jax.experimental import pallas as pl
from jax.experimental.pallas import tpu as pltpu
from jax.sharding import PartitionSpec as P

MESH = pl.DeviceIdType.MESH
LANES = 128
GROUP = 8
DEPTH = 2

DT_FLOW = 0.1
CORIOLIS = 0.3
MIXING = 0.15
COURANT = 0.24
DT_BIO = 0.5
WARMING_FACTOR = 0.5
CLEAR_WATER = 0.5


def ocean_kernel(
    dims,
    zonal_ref,
    merid_ref,
    therm_ref,
    brine_ref,
    mask_ref,
    bottom_ref,
    tracer_ref,
    sun_in,
    absorb_in,
    growth_in,
    half_in,
    light_half_in,
    stoich_in,
    east_out,
    north_out,
    warmed_out,
    salt_out,
    buoy_out,
    result_out,
    fld,
    fldh,
    mb,
    mby,
    wet,
    weth,
    den,
    denh,
    tot,
    toty,
    prs,
    prsh,
    vel,
    cour_e,
    cour_n,
    cour_p,
    cer,
    cnr,
    cpr,
    cps,
    cpack,
    mixed,
    heat,
    fin,
    q0,
    q1,
    res,
    lo,
    hi,
    hsend,
    hrecv,
    coef,
    wcol,
    warm,
    carry,
    upt,
    sun_ref,
    absorb_ref,
    growth_ref,
    half_ref,
    light_half_ref,
    stoich_ref,
    lsem,
    osem,
    p1s,
    p1r,
    cs_s,
    cs_r,
    ts_s,
    ts_r,
    as_s,
    as_r,
    qs_s,
    qs_r,
    hs_s,
    hs_r,
    ws_s,
    ws_r,
):
    ntr, levels, rows, lev, sub, ng, ny = dims
    nchunk = levels // GROUP
    nc = levels // lev
    c, g, y = lax.axis_index("comp"), lax.axis_index("gx"), lax.axis_index("gy")
    up = {
        "comp": lax.rem(c + 1, nc),
        "gx": jnp.where(c == nc - 1, lax.rem(g + 1, ng), g),
        "gy": y,
    }
    down = {
        "comp": lax.rem(c + nc - 1, nc),
        "gx": jnp.where(c == 0, lax.rem(g + ng - 1, ng), g),
        "gy": y,
    }
    gxp = {"comp": c, "gx": lax.rem(g + 1, ng), "gy": y}
    gxm = {"comp": c, "gx": lax.rem(g + ng - 1, ng), "gy": y}
    gyp = {"comp": c, "gx": g, "gy": lax.rem(y + 1, ny)}
    gym = {"comp": c, "gx": g, "gy": lax.rem(y + ny - 1, ny)}
    peers = [{"comp": lax.rem(c + d, nc), "gx": g, "gy": y} for d in range(1, nc)]

    def remote(src, dst, send, recv, device):
        return pltpu.make_async_remote_copy(
            src_ref=src,
            dst_ref=dst,
            send_sem=send,
            recv_sem=recv,
            device_id=device,
            device_id_type=MESH,
        )

    def chunk(k):
        return pl.ds(pl.multiple_of(k * GROUP, GROUP), GROUP)

    barrier = pltpu.get_barrier_semaphore()
    partners = [up, down, gxp, gxm, gyp, gym] + peers
    for peer in peers:
        p = peer["comp"]
        partners += [{**near, "comp": p} for near in (gxp, gxm, gyp, gym)]
    for device in partners:
        pl.semaphore_signal(barrier, inc=1, device_id=device, device_id_type=MESH)

    fields = (zonal_ref, merid_ref, therm_ref, brine_ref)

    def load_rows(r, _):
        for f, ref in enumerate(fields):
            pltpu.make_async_copy(ref.at[:, r, 0, :], fld.at[f, r + 1], lsem.at[f]).start()
        return 0

    lax.fori_loop(0, rows, load_rows, 0)
    for i, ref in enumerate((mask_ref, bottom_ref)):
        pltpu.make_async_copy(ref, mb.at[i, pl.ds(1, rows)], lsem.at[4 + i]).start()

    def load_tracers(k, _):
        for r in range(sub):
            pltpu.make_async_copy(
                tracer_ref.at[:, chunk(k), r, 0, :], q0.at[:, r, chunk(k), :], lsem.at[6 + k]
            ).start()
        return 0

    lax.fori_loop(0, nchunk, load_tracers, 0)
    settings = [
        pltpu.make_async_copy(src, dst, lsem.at[6 + nchunk + n])
        for n, (src, dst) in enumerate(
            (
                (sun_in, sun_ref),
                (absorb_in, absorb_ref),
                (growth_in, growth_ref),
                (half_in, half_ref),
                (light_half_in, light_half_ref),
                (stoich_in, stoich_ref),
            )
        )
    ]
    for copy in settings:
        copy.start()

    pl.semaphore_wait(barrier, len(partners))

    first = []
    for f, ref in enumerate(fields):
        first.append((ref.at[:, rows - 1, 0, :], fld.at[f, 0], gxp))
    for f in (2, 3):
        first.append((fields[f].at[:, 0, 0, :], fld.at[f, rows + 1], gxm))
    for i, ref in enumerate((mask_ref, bottom_ref)):
        first.append((ref.at[pl.ds(rows - 1, 1)], mb.at[i, pl.ds(0, 1)], gxp))
        first.append((ref.at[pl.ds(0, 1)], mb.at[i, pl.ds(rows + 1, 1)], gxm))
        first.append((ref, mby.at[0, i], gyp))
        first.append((ref, mby.at[1, i], gym))
    first = [
        remote(src, dst, p1s.at[n], p1r.at[n], device)
        for n, (src, dst, device) in enumerate(first)
    ]
    for copy in first:
        copy.start()

    def edge_copies(stage, k):
        if stage == 0:
            top = tracer_ref.at[:, chunk(k), sub - 1, 0, :]
            low = tracer_ref.at[:, chunk(k), 0, 0, :]
        else:
            top = q1.at[:, sub - 1, chunk(k), :]
            low = q1.at[:, 0, chunk(k), :]
        return (
            remote(
                top, lo.at[stage, :, chunk(k), :], qs_s.at[stage, 0, k], qs_r.at[stage, 0, k], up
            ),
            remote(
                low, hi.at[stage, :, chunk(k), :], qs_s.at[stage, 1, k], qs_r.at[stage, 1, k], down
            ),
        )

    def send_edges(stage, k):
        for copy in edge_copies(stage, k):
            copy.start()

    def side_copies(stage, k):
        return (
            remote(
                hsend.at[stage, :, chunk(k), :],
                hrecv.at[stage, 0, :, chunk(k), :],
                hs_s.at[stage, 0, k],
                hs_r.at[stage, 0, k],
                gyp,
            ),
            remote(
                hsend.at[stage, :, chunk(k), :],
                hrecv.at[stage, 1, :, chunk(k), :],
                hs_s.at[stage, 1, k],
                hs_r.at[stage, 1, k],
                gym,
            ),
        )

    def send_sides(stage, k):
        for copy in side_copies(stage, k):
            copy.start()

    for k in range(1):
        send_edges(0, k)

    lane16 = lax.broadcasted_iota(jnp.int32, (lev, LANES), 1)
    level16 = lax.broadcasted_iota(jnp.int32, (lev, LANES), 0)
    depth16 = (level16 + c * lev).astype(jnp.float32)
    lane8 = lax.broadcasted_iota(jnp.int32, (GROUP, LANES), 1)
    level8 = lax.broadcasted_iota(jnp.int32, (GROUP, LANES), 0)

    def merged(ahead, behind, lanes):
        return jnp.where((lanes & 1) == 1, ahead, pltpu.roll(behind, 2, 1))

    def slot_of(both, m):
        return pltpu.roll(both, (126 - m) % LANES, 1)

    def packed(acc, x, m, lanes):
        return jnp.where((lanes >> 1) == (m >> 1), pltpu.roll(x, (m + 1) % LANES, 1), acc)

    def ahead_of(x, h, lanes):
        return jnp.where(lanes == LANES - 1, h, pltpu.roll(x, LANES - 1, 1))

    def behind_of(x, h, lanes):
        return jnp.where(lanes == 0, h, pltpu.roll(x, 1, 1))

    for f in range(4):
        pltpu.make_async_copy(fld.at[f, pl.ds(1, rows)], fld.at[f, pl.ds(1, rows)], lsem.at[f]).wait()
    acc = jnp.zeros((lev, LANES), jnp.float32)
    for r in range(rows):
        for f in range(4):
            acc = packed(acc, fld[f, r + 1], 8 * r + 2 * f, lane16)
    cps[...] = acc
    column_copies = (
        remote(cps, cpack.at[0], cs_s.at[0], cs_r.at[0], gyp),
        remote(cps, cpack.at[1], cs_s.at[1], cs_r.at[1], gym),
    )
    for copy in column_copies:
        copy.start()

    for i, ref in enumerate((mask_ref, bottom_ref)):
        pltpu.make_async_copy(ref, mb.at[i, pl.ds(1, rows)], lsem.at[4 + i]).wait()

    def reach(m, b):
        return jnp.where(m == 1, b, 0).astype(jnp.float32)

    def wet_row(e, valid):
        depth = reach(mb[0, e], mb[1, e])
        if valid is not None:
            depth = jnp.where(valid, depth, 0.0)
        w = jnp.where(depth16 < depth, 1.0, 0.0)
        d = w * (-0.2 * fld[2, e] + 0.8 * fld[3, e])
        wet[e] = w
        den[e] = d
        tot[c, e] = jnp.sum(d, axis=0, keepdims=True)

    def own_row(r, _):
        wet_row(r + 1, None)
        return 0

    lax.fori_loop(0, rows, own_row, 0)

    def total_copies(source, p):
        whole = tot.at[source, pl.ds(1, rows)]
        sends = (
            (whole, whole, {"gx": g, "gy": y}),
            (tot.at[source, pl.ds(rows, 1)], tot.at[source, pl.ds(0, 1)], gxp),
            (tot.at[source, pl.ds(1, 1)], tot.at[source, pl.ds(rows + 1, 1)], gxm),
            (whole, toty.at[0, source], gyp),
            (whole, toty.at[1, source], gym),
        )
        return [
            remote(src, dst, ts_s.at[n, p], ts_r.at[n, source], {**device, "comp": p})
            for n, (src, dst, device) in enumerate(sends)
        ]

    for p in range(1, nc):

        @pl.when(p > c)
        def _(p=p):
            for copy in total_copies(c, p):
                copy.start()

    def pack_chunk(stage, src, k):
        for pair in range(sub // 2):
            a = jnp.zeros((GROUP, LANES), jnp.float32)
            for half in range(2):
                for t in range(ntr):
                    a = packed(a, src[t, 2 * pair + half, chunk(k), :], 64 * half + 2 * t, lane8)
            hsend[stage, pair, chunk(k), :] = a

    def pack_sides(k, _):
        pltpu.make_async_copy(
            q0.at[:, :, chunk(k), :], q0.at[:, :, chunk(k), :], lsem.at[6 + k]
        ).wait()
        pack_chunk(0, q0, k)
        return 0

    lax.fori_loop(0, nchunk, pack_sides, 0)

    for copy in first:
        copy.wait_recv()
    for copy in column_copies:
        copy.wait_recv()
    wet_row(0, g > 0)
    wet_row(rows + 1, g < ng - 1)
    both = merged(cpack[1], cpack[0], lane16)
    for r in range(rows):
        for f in range(4):
            fldh[f, r] = slot_of(both, 8 * r + 2 * f)

    def halo_columns(r, _):
        behind = jnp.broadcast_to(reach(mby[0, 0, r], mby[0, 1, r]), (lev, LANES))
        ahead = jnp.broadcast_to(reach(mby[1, 0, r], mby[1, 1, r]), (lev, LANES))
        behind = jnp.where(y > 0, pltpu.roll(behind, 1, 1), 0.0)
        ahead = jnp.where(y < ny - 1, pltpu.roll(ahead, LANES - 1, 1), 0.0)
        depth = jnp.where(lane16 == 0, behind, ahead)
        w = jnp.where(depth16 < depth, 1.0, 0.0)
        d = w * (-0.2 * fldh[2, r] + 0.8 * fldh[3, r])
        weth[r] = w
        denh[r] = d
        return 0

    lax.fori_loop(0, rows, halo_columns, 0)

    for k in range(1, 2):
        send_edges(0, k)

    for p in range(nc - 1):

        @pl.when(p < c)
        def _(p=p):
            for copy in total_copies(p, p):
                copy.wait_recv()

    def running(d):
        incl = d
        step = 1
        while step < lev:
            incl = incl + jnp.where(level16 >= step, pltpu.roll(incl, step, 0), 0.0)
            step *= 2
        return incl - 0.5 * d

    def levels_above(totals):
        offset = jnp.zeros((1, LANES), jnp.float32)
        for p in range(nc - 1):
            offset = offset + jnp.where(p < c, totals(p), 0.0)
        return jnp.broadcast_to(offset, (lev, LANES))

    def pressure_row(e, _):
        prs[e] = levels_above(lambda p: tot[p, e]) + running(den[e])
        return 0

    def pressure_column(r, _):
        behind = pltpu.roll(levels_above(lambda p: toty[0, p, r]), 1, 1)
        ahead = pltpu.roll(levels_above(lambda p: toty[1, p, r]), LANES - 1, 1)
        prsh[r] = jnp.where(lane16 == 0, behind, ahead) + running(denh[r])
        return 0

    lax.fori_loop(0, rows + 2, pressure_row, 0)
    lax.fori_loop(0, rows, pressure_column, 0)

    def east_row(e, _):
        v = (wet[e] * wet[e + 1]) * (
            fld[0, e] + DT_FLOW * (CORIOLIS * fld[1, e] - (prs[e + 1] - prs[e]))
        )
        vel[0, e] = v
        cour_e[e] = COURANT * jnp.tanh(v)
        return 0

    lax.fori_loop(0, rows + 1, east_row, 0)

    def north_group(p, _):
        pack = jnp.zeros((lev, LANES), jnp.float32)
        for i in range(sub):
            r = sub * p + i
            w, h, ps, ph = wet[r + 1], weth[r], prs[r + 1], prsh[r]
            v = (w * ahead_of(w, h, lane16)) * (
                fld[1, r + 1]
                + DT_FLOW * (-CORIOLIS * fld[0, r + 1] - (ahead_of(ps, ph, lane16) - ps))
            )
            vel[1, r + 1] = v
            cour_n[r] = COURANT * jnp.tanh(v)
            before = (w * h) * (
                fldh[1, r] + DT_FLOW * (-CORIOLIS * fldh[0, r] - (ps - ph))
            )
            pack = jnp.where(
                lane16 == i, jnp.broadcast_to(before[:, 0:1], (lev, LANES)), pack
            )
        cour_p[p] = COURANT * jnp.tanh(pack)
        return 0

    lax.fori_loop(0, nc, north_group, 0)

    mine = pl.ds(pl.multiple_of(c * lev, lev), lev)
    velocity_copies = []
    for d, peer in enumerate(peers):
        p = peer["comp"]
        for n, (src, dst) in enumerate(
            (
                (cour_e.at[pl.ds(sub * p, sub + 1)], cer.at[:, mine, :]),
                (cour_n.at[pl.ds(sub * p, sub)], cnr.at[:, mine, :]),
                (cour_p.at[p], cpr.at[mine, :]),
            )
        ):
            velocity_copies.append(remote(src, dst, as_s.at[d, n], as_r.at[d, n], peer))
    for copy in velocity_copies:
        copy.start()
    for k in range(2):
        send_sides(0, k)
    for i in range(sub + 1):
        cer[i, mine, :] = cour_e[sub * c + i]
    for i in range(sub):
        cnr[i, mine, :] = cour_n[sub * c + i]
    cpr[mine, :] = cour_p[c]

    def mixing_row(r, _):
        w, h = wet[r + 1], weth[r]
        open_e, open_w = w * wet[r + 2], wet[r] * w
        open_n, open_s = w * ahead_of(w, h, lane16), w * behind_of(w, h, lane16)
        for i in range(2):
            x, xh = fld[2 + i, r + 1], fldh[2 + i, r]
            flux_e = open_e * (fld[2 + i, r + 2] - x)
            flux_w = open_w * (x - fld[2 + i, r])
            flux_n = open_n * (ahead_of(x, xh, lane16) - x)
            flux_s = open_s * (x - behind_of(x, xh, lane16))
            mixed[i, r] = x + MIXING * ((flux_e - flux_w) + (flux_n - flux_s))
        return 0

    lax.fori_loop(0, rows, mixing_row, 0)

    def store_rows(r, _):
        pltpu.make_async_copy(vel.at[0, r + 1], east_out.at[:, r, 0, :], osem.at[0]).start()
        pltpu.make_async_copy(vel.at[1, r + 1], north_out.at[:, r, 0, :], osem.at[1]).start()
        pltpu.make_async_copy(mixed.at[1, r], salt_out.at[:, r, 0, :], osem.at[2]).start()
        return 0

    lax.fori_loop(0, rows, store_rows, 0)

    for copy in velocity_copies:
        copy.wait_recv()

    def wet_chunk(k, r):
        depth = reach(mb[0, sub * c + r + 1], mb[1, sub * c + r + 1])
        return jnp.where((level8 + k * GROUP).astype(jnp.float32) < depth, 1.0, 0.0)

    def coefficients(k):
        for r in range(sub):
            ce, cw, cn = cer[r + 1, chunk(k), :], cer[r, chunk(k), :], cnr[r, chunk(k), :]
            edge = cpr[chunk(k), :]
            if r:
                edge = pltpu.roll(edge, LANES - r, 1)
            cs = behind_of(cn, edge, lane8)
            w = wet_chunk(k, r)
            out_e, in_e = jnp.maximum(ce, 0.0), jnp.minimum(ce, 0.0)
            out_w, in_w = jnp.maximum(cw, 0.0), jnp.minimum(cw, 0.0)
            out_n, in_n = jnp.maximum(cn, 0.0), jnp.minimum(cn, 0.0)
            out_s, in_s = jnp.maximum(cs, 0.0), jnp.minimum(cs, 0.0)
            wcol[r, chunk(k), :] = w
            coef[0, r, chunk(k), :] = w * (1.0 - (out_e - in_w) - (out_n - in_s))
            coef[1, r, chunk(k), :] = -w * in_e
            coef[2, r, chunk(k), :] = w * out_w
            coef[3, r, chunk(k), :] = -w * in_n
            coef[4, r, chunk(k), :] = w * out_s

    def substep(k, src, dst, stage, each):
        cf = [[coef[i, r, chunk(k), :] for i in range(5)] for r in range(sub)]
        both = [
            merged(hrecv[stage, 1, p, chunk(k), :], hrecv[stage, 0, p, chunk(k), :], lane8)
            for p in range(sub // 2)
        ]
        for t in range(ntr):
            q = [lo[stage, t, chunk(k), :]]
            q += [src[t, r, chunk(k), :] for r in range(sub)]
            q += [hi[stage, t, chunk(k), :]]
            for r in range(sub):
                x = q[r + 1]
                h = slot_of(both[r // 2], 64 * (r % 2) + 2 * t)
                new = (
                    cf[r][0] * x
                    + cf[r][1] * q[r + 2]
                    + cf[r][2] * q[r]
                    + cf[r][3] * ahead_of(x, h, lane8)
                    + cf[r][4] * behind_of(x, h, lane8)
                )
                dst[t, r, chunk(k), :] = new
                each(t, r, new)

    def first_substep(k):
        for copy in edge_copies(0, k):
            copy.wait_recv()
        for copy in side_copies(0, k):
            copy.wait_recv()
        coefficients(k)
        substep(k, q0, q1, 0, lambda t, r, new: None)
        send_edges(1, k)
        pack_chunk(1, q1, k)
        send_sides(1, k)

        @pl.when(k + DEPTH < nchunk)
        def _():
            send_sides(0, k + DEPTH)
            send_edges(0, k + DEPTH)


    for copy in settings:
        copy.wait()
    layer = 2.0 / levels
    block = 4
    carry[...] = jnp.zeros_like(carry)

    def second_substep(k):
        for copy in edge_copies(1, k):
            copy.wait_recv()
        for copy in side_copies(1, k):
            copy.wait_recv()
        optical = [jnp.zeros((GROUP, LANES), jnp.float32) for _ in range(sub)]

        def each(t, r, new):
            optical[r] = optical[r] + absorb_ref[t] * new

        substep(k, q1, q0, 1, each)
        light, scaled, nutrient = [], [], []
        for r in range(sub):
            step = layer * (CLEAR_WATER + optical[r])
            above = jnp.where(level8 >= 1, pltpu.roll(step, 1, 0), 0.0)
            for d in (1, 2, 4):
                above = above + jnp.where(level8 >= d, pltpu.roll(above, d, 0), 0.0)
            before = carry[r]
            carry[r] = before + jnp.sum(step, axis=0, keepdims=True)
            arriving = sun_ref[r] * jnp.exp(-(before + above))
            warm[r, chunk(k), :] = (
                wcol[r, chunk(k), :] * arriving * (1.0 - jnp.exp(-step)) / layer
            )
            light.append(arriving * jnp.exp(-0.5 * step))
            nutrient.append(q0[0, r, chunk(k), :])
            scaled.append(nutrient[r] * light[r])
        for t in range(ntr):
            for r in range(sub):
                below = (half_ref[t] + nutrient[r]) * (light[r] + light_half_ref[t])
                upt[t, r] = (growth_ref[t] * scaled[r]) * q0[t, r, chunk(k), :] / below
        half_wet = [DT_BIO * wcol[r, chunk(k), :] for r in range(sub)]

        def react(b, _):
            sums = [[jnp.zeros((GROUP, LANES), jnp.float32)] * sub for _ in range(block)]
            for t in range(ntr):
                u = [upt[t, r] for r in range(sub)]
                for i in range(block):
                    s = stoich_ref[block * b + i, t]
                    sums[i] = [sums[i][r] + s * u[r] for r in range(sub)]
            for i in range(block):
                for r in range(sub):
                    res[block * b + i, r, chunk(k), :] = (
                        q0[block * b + i, r, chunk(k), :] + half_wet[r] * sums[i][r]
                    )
            return 0

        lax.fori_loop(0, ntr // block, react, 0)
        for r in range(sub):
            pltpu.make_async_copy(
                res.at[:, r, chunk(k), :], result_out.at[:, chunk(k), r, 0, :], osem.at[3]
            ).start()

    def heat_copy(p):
        part = pl.ds(pl.multiple_of(p * lev, lev), lev)
        return remote(
            warm.at[:, part, :],
            heat.at[pl.ds(sub * c, sub)],
            ws_s.at[p],
            ws_r.at[c],
            {"comp": p, "gx": g, "gy": y},
        )

    def send_heat(p):
        @pl.when(p != c)
        def _():
            heat_copy(p).start()

        @pl.when(p == c)
        def _():
            part = pl.ds(pl.multiple_of(p * lev, lev), lev)
            for r in range(sub):
                heat[sub * c + r] = warm[r, part, :]

    each_peer = lev // GROUP

    def advance(k, _):
        @pl.when(k < nchunk)
        def _():
            first_substep(k)

        @pl.when(k > 0)
        def _():
            second_substep(k - 1)

        @pl.when((k > 0) & (lax.rem(k, each_peer) == 0))
        def _():
            send_heat(k // each_peer - 1)

        return 0

    lax.fori_loop(0, nchunk + 1, advance, 0)

    for d in range(1, nc):
        p = lax.rem(c + nc - d, nc)
        remote(
            warm.at[:, pl.ds(0, lev), :],
            heat.at[pl.ds(sub * p, sub)],
            ws_s.at[p],
            ws_r.at[p],
            {"comp": p, "gx": g, "gy": y},
        ).wait_recv()

    def final_row(r, _):
        warmed = mixed[0, r] + WARMING_FACTOR * heat[r]
        fin[0, r] = warmed
        fin[1, r] = wet[r + 1] * (0.2 * warmed - 0.8 * mixed[1, r])
        return 0

    lax.fori_loop(0, rows, final_row, 0)

    def store_final(r, _):
        pltpu.make_async_copy(fin.at[0, r], warmed_out.at[:, r, 0, :], osem.at[4]).start()
        pltpu.make_async_copy(fin.at[1, r], buoy_out.at[:, r, 0, :], osem.at[5]).start()
        return 0

    lax.fori_loop(0, rows, store_final, 0)

    for copy in first + list(column_copies) + velocity_copies:
        copy.wait_send()
    for p in range(1, nc):

        @pl.when(p > c)
        def _(p=p):
            for copy in total_copies(c, p):
                copy.wait_send()

    def drain(k, _):
        for stage in range(2):
            for copy in edge_copies(stage, k) + side_copies(stage, k):
                copy.wait_send()
        return 0

    lax.fori_loop(0, nchunk, drain, 0)
    for d in range(1, nc):
        heat_copy(lax.rem(c + d, nc)).wait_send()
    for n, ref in enumerate(
        (vel.at[0, pl.ds(1, rows)], vel.at[1, pl.ds(1, rows)], mixed.at[1], res, fin.at[0], fin.at[1])
    ):
        pltpu.make_async_copy(ref, ref, osem.at[n]).wait()


def place_kernel(count, *refs):
    sources, targets = refs[:count], refs[count : 2 * count]
    held, sems = refs[2 * count : 3 * count], refs[3 * count]
    copies = []
    for n in range(count):
        parts = 8 if n == count - 1 else 1
        size = sources[n].shape[0] // parts
        for p in range(parts):
            part = pl.ds(p * size, size)
            copies.append(
                (
                    pltpu.make_async_copy(
                        sources[n].at[part], held[n].at[part], sems.at[0, n, p]
                    ),
                    pltpu.make_async_copy(
                        held[n].at[part], targets[n].at[part], sems.at[1, n, p]
                    ),
                )
            )
    copies = copies[count - 1 :] + copies[: count - 1]
    for fetch, _ in copies:
        fetch.start()
    for fetch, put in copies:
        fetch.wait()
        put.start()
    for _, put in copies:
        put.wait()


def on_device(mesh_shape, *args):
    (
        zonal,
        merid,
        therm,
        brine,
        mask,
        bottom,
        tracers,
        sun,
        absorb,
        growth,
        half,
        light_half,
        stoich,
    ) = args
    lev, rows, lanes = zonal.shape
    ntr, levels, sub = tracers.shape[0], tracers.shape[1], tracers.shape[4]
    nc, ng, ny = mesh_shape
    nchunk = levels // GROUP
    f32, i32 = jnp.float32, jnp.int32
    column = (lev, rows, 1, lanes)
    vm, dma = pltpu.VMEM, pltpu.SemaphoreType.DMA
    anywhere = pl.BlockSpec(memory_space=pl.ANY)
    scratch = [
        vm((4, rows + 2, lev, lanes), f32),
        vm((4, rows, lev, lanes), f32),
        vm((2, rows + 2, 1, lanes), i32),
        vm((2, 2, rows, 1, lanes), i32),
        vm((rows + 2, lev, lanes), f32),
        vm((rows, lev, lanes), f32),
        vm((rows + 2, lev, lanes), f32),
        vm((rows, lev, lanes), f32),
        vm((nc, rows + 2, 1, lanes), f32),
        vm((2, nc, rows, 1, lanes), f32),
        vm((rows + 2, lev, lanes), f32),
        vm((rows, lev, lanes), f32),
        vm((2, rows + 1, lev, lanes), f32),
        vm((rows + 1, lev, lanes), f32),
        vm((rows, lev, lanes), f32),
        vm((nc, lev, lanes), f32),
        vm((sub + 1, levels, lanes), f32),
        vm((sub, levels, lanes), f32),
        vm((levels, lanes), f32),
        vm((lev, lanes), f32),
        vm((2, lev, lanes), f32),
        vm((2, rows, lev, lanes), f32),
        vm((rows, lev, lanes), f32),
        vm((2, rows, lev, lanes), f32),
        vm((ntr, sub, levels, lanes), f32),
        vm((ntr, sub, levels, lanes), f32),
        vm((ntr, sub, levels, lanes), f32),
        vm((2, ntr, levels, lanes), f32),
        vm((2, ntr, levels, lanes), f32),
        vm((2, sub // 2, levels, lanes), f32),
        vm((2, 2, sub // 2, levels, lanes), f32),
        vm((5, sub, levels, lanes), f32),
        vm((sub, levels, lanes), f32),
        vm((sub, levels, lanes), f32),
        vm((sub, GROUP, lanes), f32),
        vm((ntr, sub, GROUP, lanes), f32),
        vm((sub, 1, lanes), f32),
        pltpu.SMEM((ntr,), f32),
        pltpu.SMEM((ntr,), f32),
        pltpu.SMEM((ntr,), f32),
        pltpu.SMEM((ntr,), f32),
        pltpu.SMEM((ntr, ntr), f32),
        dma((12 + nchunk,)),
        dma((6,)),
        dma((14,)),
        dma((14,)),
        dma((2,)),
        dma((2,)),
        dma((5, nc)),
        dma((5, nc)),
        dma((nc - 1, 3)),
        dma((nc - 1, 3)),
        dma((2, 2, nchunk)),
        dma((2, 2, nchunk)),
        dma((2, 2, nchunk)),
        dma((2, 2, nchunk)),
        dma((nc,)),
        dma((nc,)),
    ]
    outs = pl.pallas_call(
        functools.partial(ocean_kernel, (ntr, levels, rows, lev, sub, ng, ny)),
        out_shape=[jax.ShapeDtypeStruct(column, f32)] * 5
        + [jax.ShapeDtypeStruct((ntr, levels, sub, 1, lanes), f32)],
        in_specs=[anywhere] * 13,
        out_specs=[anywhere] * 6,
        scratch_shapes=scratch,
        compiler_params=pltpu.CompilerParams(
            collective_id=0, has_side_effects=True, vmem_limit_bytes=67043328
        ),
        name="ocean",
    )(
        *(x.reshape(column) for x in (zonal, merid, therm, brine)),
        mask.reshape(rows, 1, lanes),
        bottom.reshape(rows, 1, lanes),
        tracers.reshape(ntr, levels, sub, 1, lanes),
        sun.reshape(sub, 1, lanes),
        absorb,
        growth,
        half,
        light_half,
        stoich,
    )
    outs = [x.reshape(zonal.shape) for x in outs[:5]] + [outs[5].reshape(tracers.shape)]
    count = len(outs)
    return tuple(
        pl.pallas_call(
            functools.partial(place_kernel, count),
            out_shape=[jax.ShapeDtypeStruct(x.shape, f32) for x in outs],
            in_specs=[anywhere] * count,
            out_specs=[anywhere] * count,
            scratch_shapes=[vm(x.shape, f32) for x in outs] + [dma((2, count, 8))],
            compiler_params=pltpu.CompilerParams(vmem_limit_bytes=67043328),
            name="place",
        )(*outs)
    )


def solution(mesh):
    field = P("comp", "gx", "gy")
    tile = P("gx", "gy")
    tracer = P(None, None, "gx", "comp", None, "gy")
    shape = tuple(mesh.shape[a] for a in ("comp", "gx", "gy"))
    return jax.shard_map(
        functools.partial(on_device, shape),
        mesh=mesh,
        in_specs=(field,) * 4 + (tile,) * 2 + (tracer, P("gx", "comp", None, "gy")) + (P(),) * 5,
        out_specs=(field,) * 5 + (tracer,),
        check_vma=False,
    )
```
